512 devices in a mesh: gx: 16 (over z), gy: 4 (over x), gz: 8 (over y, core).
Axes of the slice: x: 4, y: 4, z: 16, core: 2. Of those that a mesh axis runs over, the one named last changes fastest.
Arguments:
- flow: float32 [4, 128, 64, 1024], P(None, 'gx', 'gy', 'gz'), may hold values from -3 to 3
- basis: float32 [127, 3, 131072], P(None, None, ('gx', 'gy', 'gz')), may hold values from -1150 to 1150
- sample: int32 [131072], P(('gx', 'gy', 'gz')), may hold values from 0 to 16383
Outputs:
- flow_next: float32 [4, 128, 64, 1024], P(None, 'gx', 'gy', 'gz')
- basis_next: float32 [128, 3, 131072], P(None, None, ('gx', 'gy', 'gz'))
- factor: float32 [128, 128], replicated
The draws below stay inside these ranges and needn't reach their ends.
All inputs are finite; a program needn't handle non-finite values.
Results may differ from the reference program's by a relative error of at most 0.000065.
Values sent between devices are 32-bit elements; how exact they have to be, the bound alone decides.
A program may use at most 64 MiB of HBM per device.

```python
import math
import jax
import jax.numpy as jnp
from jax import lax

CX = 8
CY = 16
CZ = 128
PTS_DEV = 256
MODES = 127
NX = 128
NY = 64
NZ = 1024
POINTS = 131072
N_GY = 4
N_GZ = 8


def draw_basis(key, part):
    first, second, third = jax.random.split(key, 3)
    base = jnp.clip(jax.random.normal(first, (MODES, 3, POINTS), jnp.float32), -6.0, 6.0)
    top = math.log(10.0)
    mixed = base + 0.3 * jnp.roll(base, 1, axis=0) + 0.2 * jnp.roll(base, 5, axis=0)
    column = jnp.exp(jax.random.uniform(second, (MODES, 1, 1), jnp.float32, 0.0, math.log(10.0)))
    blocks = POINTS // PTS_DEV
    rising = jnp.arange(blocks, dtype=jnp.float32) / max(blocks - 1, 1)
    spread = jax.random.uniform(third, (blocks,), jnp.float32)
    row_scale = jnp.repeat(jnp.exp(top * (0.5 * rising + 0.5 * spread)), PTS_DEV)
    return mixed * column * row_scale[None, None, :]


def set_ends(result, rng, smallest, high):
    longest = result.shape.index(max(result.shape))
    spots = []
    for shift in (0, 1):
        where = [jax.random.randint(jax.random.fold_in(rng, axis), (), 0, length) for axis, length in enumerate(result.shape)]
        where[longest] = (where[longest] + shift) % result.shape[longest]
        spots.append(tuple(where))
    return result.at[spots[0]].set(smallest).at[spots[1]].set(high)


def shard_levels(stream_key, shape, cuts, low, high):
    level = 1.0
    for dim, blocks in cuts:
        heights = jax.random.uniform(jax.random.fold_in(jax.random.fold_in(stream_key, 6), dim), (blocks,), jnp.float32, low / len(cuts), high / len(cuts))
        level = level * jnp.repeat(jnp.exp(heights), shape[dim] // blocks).reshape((-1,) + (1,) * (len(shape) - 1 - dim))
    return level


def scatter_about(stream_key, shape, width, bound, cuts=(), held_as=jnp.bfloat16):
    factor_of = shard_levels(stream_key, shape, cuts, -0.22, 0.18) if cuts else 1.0
    values = jax.random.normal(stream_key, shape, jnp.float32) * width * factor_of
    return jnp.minimum(jnp.maximum(values, -bound), bound).astype(held_as)


def setup_inputs(seed: int = 0) -> dict:
    seeds = jax.random.split(jax.random.key(seed), 4)
    flow = scatter_about(seeds[0], (4, NX, NY, NZ), 0.5, 3.0, ((1, 16), (2, 4), (3, 8)), jnp.float32)
    basis = draw_basis(jax.random.fold_in(seeds[3], 71), 0)
    sample = set_ends(jax.random.randint(seeds[2], (POINTS,), 0, CX * CY * CZ), jax.random.fold_in(seeds[2], 1), 0, (CX * CY * CZ) - 1).astype(jnp.int32)
    return dict(flow=flow, basis=basis, sample=sample)


DT_STEP = 0.35
VISCOSITY = 0.2
SOUND_SQ = 1.0
DRIVING = 0.5

def rates(ext):
    centre = ext[:, 1:-1, 1:-1, 1:-1]
    x_plus = ext[:, 2:, 1:-1, 1:-1]
    x_minus = ext[:, :-2, 1:-1, 1:-1]
    y_plus = ext[:, 1:-1, 2:, 1:-1]
    y_minus = ext[:, 1:-1, :-2, 1:-1]
    z_plus = ext[:, 1:-1, 1:-1, 2:]
    z_minus = ext[:, 1:-1, 1:-1, :-2]
    slope_x = 0.5 * (x_plus - x_minus)
    slope_y = 0.5 * (y_plus - y_minus)
    slope_z = 0.5 * (z_plus - z_minus)
    laplace = x_plus + x_minus + (y_plus + y_minus) + (z_plus + z_minus) - 6.0 * centre
    advect = centre[0] * slope_x[:3] + centre[1] * slope_y[:3] + centre[2] * slope_z[:3]
    pressure = jnp.stack([slope_x[3], slope_y[3], slope_z[3]])
    forcing = jnp.array([DRIVING, 0.0, 0.0], dtype=jnp.float32).reshape(3, 1, 1, 1)
    velocity = VISCOSITY * laplace[:3] - advect - pressure + forcing
    density = -SOUND_SQ * (slope_x[0] + slope_y[1] + slope_z[2])
    return jnp.concatenate([velocity, density[None]], axis=0)

def extend(fields):
    walled = jnp.pad(fields, ((0, 0), (0, 0), (1, 1), (0, 0)))
    return jnp.pad(walled, ((0, 0), (1, 1), (0, 0), (1, 1)), mode='wrap')

def reference(flow, basis, sample):
    section_one = flow + DT_STEP * rates(extend(flow))
    section_two = 0.75 * flow + 0.25 * (section_one + DT_STEP * rates(extend(section_one)))
    flow_next = 1.0 / 3.0 * flow + 2.0 / 3.0 * (section_two + DT_STEP * rates(extend(section_two)))
    rows = jnp.arange(POINTS, dtype=jnp.int32)
    brick = rows // PTS_DEV
    brick_x = brick // (N_GY * N_GZ)
    brick_y = brick // N_GZ % N_GY
    brick_z = brick % N_GZ
    cell_x = brick_x * CX + sample // (CY * CZ)
    cell_y = brick_y * CY + sample // CZ % CY
    cell_z = brick_z * CZ + sample % CZ
    snapshot = flow_next[:3, cell_x, cell_y, cell_z]
    stacked = jnp.concatenate([basis, snapshot[None]], axis=0).reshape(MODES + 1, 3 * POINTS)
    gram = jnp.dot(stacked.astype(jnp.float32), stacked.T.astype(jnp.float32), precision=lax.Precision.HIGHEST, preferred_element_type=jnp.float32) / (3.0 * POINTS)
    lower = jnp.linalg.cholesky(gram)
    basis_next = jax.scipy.linalg.solve_triangular(lower, stacked, lower=True).reshape(MODES + 1, 3, POINTS)
    return (flow_next, basis_next, lower.T)
```

```python
import jax
import jax.numpy as jnp
from jax import lax
from jax.experimental import pallas as pl
from jax.experimental.pallas import tpu as pltpu
from jax.sharding import PartitionSpec as P

DT_STEP = 0.35
VISCOSITY = 0.2
SOUND_SQ = 1.0
DRIVING = 0.5
GX, GY, GZ = 16, 4, 8
PLANE = GY * GZ
COUNT = 3.0 * 256 * GX * GY * GZ
MESH = pl.DeviceIdType.MESH
HIGH = lax.Precision.HIGHEST
F32 = jnp.float32


def iota(shape, dim):
    return lax.broadcasted_iota(jnp.int32, shape, dim)


def stencil(field, flow, out, ylo, yhi, zlo, zhi, ynext, gy, weights):
    lane = iota((16, 128), 1)
    lane8 = iota((8, 128), 1)
    row = iota((16, 128), 0)
    low_z, high_z = zlo[...], zhi[...]

    def body(x, faces):
        zl = pltpu.roll(low_z, 64 - 8 * x, 1)
        zh = pltpu.roll(high_z, lax.rem(128 - 8 * x, 128), 1)
        mid = [field[c, x + 1] for c in range(4)]
        sx, sy, sz, lap = [], [], [], []
        for c in range(4):
            a = mid[c]
            xp, xm = field[c, x + 2], field[c, x]
            above = jnp.where(gy < GY - 1, yhi[c, pl.ds(x, 1), :], 0.0)
            below = jnp.where(gy > 0, ylo[c, pl.ds(x, 1), :], 0.0)
            yp = jnp.where(row == 15, above, pltpu.roll(a, 15, 0))
            ym = jnp.where(row == 0, below, pltpu.roll(a, 1, 0))
            m = 2 * c
            left = jnp.concatenate([zl[:, m:m + 1], zl[:, m + 1:m + 2]], axis=0)
            right = jnp.concatenate([zh[:, m:m + 1], zh[:, m + 1:m + 2]], axis=0)
            zp = jnp.where(lane == 127, right, pltpu.roll(a, 127, 1))
            zm = jnp.where(lane == 0, left, pltpu.roll(a, 1, 1))
            sx.append(0.5 * (xp - xm))
            sy.append(0.5 * (yp - ym))
            sz.append(0.5 * (zp - zm))
            if c < 3:
                lap.append(xp + xm + (yp + ym) + (zp + zm) - 6.0 * a)
        press = (sx[3], sy[3], sz[3])
        for c in range(4):
            if c < 3:
                rate = (VISCOSITY * lap[c] - (mid[0] * sx[c] + mid[1] * sy[c] + mid[2] * sz[c])
                        - press[c])
                if c == 0:
                    rate = rate + DRIVING
            else:
                rate = -SOUND_SQ * (sx[0] + sy[1] + sz[2])
            new = mid[c] + DT_STEP * rate
            if weights is not None:
                new = weights[0] * flow[c, x + 1] + weights[1] * new
            if ynext is None:
                out[c, x] = new
            else:
                out[c, x + 1] = new
                faces = pack(new, c, x, faces, lane8, ynext)
        return faces

    return lax.fori_loop(0, 8, body, jnp.zeros((8, 128), F32))


def pack(new, c, x, faces, lane8, ynext):
    ynext[0, c, pl.ds(x, 1), :] = new[0:1]
    ynext[1, c, pl.ds(x, 1), :] = new[15:16]
    for half in range(2):
        tile = new[8 * half:8 * half + 8]
        spot = 8 * x + 2 * c + half
        faces = jnp.where(lane8 == spot, tile[:, 0:1], faces)
        faces = jnp.where(lane8 == spot + 64, tile[:, 127:128], faces)
    return faces


def comm_kernel(flow, bt, sample, out, snap_out, gram_out, row_out,
                fields, ysend, zsend, ylo, yhi, zlo, zhi,
                scat, r1, piece, r2, mine, full, rowmine, rr1, rowsum, rr2,
                load_sem, ssem, rsem, gsem):
    gx, gy, gz = (lax.axis_index(n) for n in ("gx", "gy", "gz"))
    me = gy * GZ + gz

    def plane_id(k):
        other = lax.rem(me + k, PLANE)
        return other, (gx, other // GZ, lax.rem(other, GZ))

    def line_id(k):
        return (lax.rem(gx + k, GX), gy, gz)

    load = pltpu.make_async_copy(flow, fields.at[0, :, pl.ds(1, 8)], load_sem)
    load.start()
    barrier = pltpu.get_barrier_semaphore()

    def greet_plane(k, carry):
        pl.semaphore_signal(barrier, inc=1, device_id=plane_id(k)[1], device_id_type=MESH)
        return carry

    def greet_line(k, carry):
        pl.semaphore_signal(barrier, inc=1, device_id=line_id(k), device_id_type=MESH)
        return carry

    lax.fori_loop(1, GX, greet_line, 0)
    lax.fori_loop(1, PLANE, greet_plane, 0)

    gram = jnp.zeros((128, 128), F32)
    for c in range(3):
        gram = gram + lax.dot_general(bt[c], bt[c], (((1,), (1,)), ((), ())), precision=HIGH,
                                      preferred_element_type=F32)
    for i in range(PLANE):
        scat[i] = gram[4 * i:4 * i + 4]

    load.wait()
    lane8 = iota((8, 128), 1)

    def first(x, faces):
        for c in range(4):
            faces = pack(fields[0, c, x + 1], c, x, faces, lane8, ysend.at[0])
        return faces

    zsend[0] = lax.fori_loop(0, 8, first, jnp.zeros((8, 128), F32))
    pl.semaphore_wait(barrier, GX - 1 + PLANE - 1)

    right = {
        "gx": (lax.rem(gx + 1, GX), gy, gz), "gy": (gx, lax.rem(gy + 1, GY), gz),
        "gz": (gx, gy, lax.rem(gz + 1, GZ)),
    }
    left = {
        "gx": (lax.rem(gx + GX - 1, GX), gy, gz), "gy": (gx, lax.rem(gy + GY - 1, GY), gz),
        "gz": (gx, gy, lax.rem(gz + GZ - 1, GZ)),
    }

    def exchange(s):
        f = fields.at[s]
        moves = [
            (f.at[:, pl.ds(1, 1)], f.at[:, pl.ds(9, 1)], left["gx"]),
            (f.at[:, pl.ds(8, 1)], f.at[:, pl.ds(0, 1)], right["gx"]),
            (ysend.at[s, 0], yhi.at[s], left["gy"]),
            (ysend.at[s, 1], ylo.at[s], right["gy"]),
            (zsend.at[s], zhi.at[s], left["gz"]),
            (zsend.at[s], zlo.at[s], right["gz"]),
        ]
        copies = [
            pltpu.make_async_remote_copy(src_ref=a, dst_ref=b, send_sem=ssem.at[s, i],
                                         recv_sem=rsem.at[s, i], device_id=d, device_id_type=MESH)
            for i, (a, b, d) in enumerate(moves)
        ]
        for copy in copies:
            copy.start()
        return copies

    def scatter(k, carry):
        other, where = plane_id(k)
        pltpu.make_async_remote_copy(src_ref=scat.at[other], dst_ref=r1.at[me], send_sem=gsem.at[0],
                                     recv_sem=gsem.at[1], device_id=where, device_id_type=MESH).start()
        return carry

    def spread(src, dst, sems, line):
        def go(k, carry):
            where = line_id(k) if line else plane_id(k)[1]
            pltpu.make_async_remote_copy(src_ref=src, dst_ref=dst.at[gx if line else me],
                                         send_sem=gsem.at[sems], recv_sem=gsem.at[sems + 1],
                                         device_id=where, device_id_type=MESH).start()
            return carry
        lax.fori_loop(1, GX if line else PLANE, go, 0)

    def settle(buf, sem, count):
        part = buf.at[pl.ds(0, count)]
        pltpu.make_async_copy(part, part, gsem.at[sem]).wait()

    def step(s, dst, weights):
        ynext = ysend.at[s + 1] if s < 2 else None
        faces = stencil(fields.at[s], fields.at[0], dst, ylo.at[s], yhi.at[s], zlo.at[s],
                        zhi.at[s], ynext, gy, weights)
        if s < 2:
            zsend[s + 1] = faces

    copies = exchange(0)
    everything = list(copies)
    lax.fori_loop(1, PLANE, scatter, 0)
    r1[me] = scat[me]
    for c in copies:
        c.wait_recv()
    step(0, fields.at[1], None)
    copies = exchange(1)
    everything += copies

    settle(r1, 1, PLANE - 1)
    total = r1[0]
    for i in range(1, PLANE):
        total = total + r1[i]
    piece[...] = total
    spread(piece, r2, 2, True)
    r2[gx] = total

    for c in copies:
        c.wait_recv()
    step(1, fields.at[2], (0.75, 0.25))
    copies = exchange(2)
    everything += copies
    for c in copies:
        c.wait_recv()
    step(2, out, (1.0 / 3.0, 2.0 / 3.0))

    s = sample[...]
    rows = (iota((128, 256), 0) == s // 128).astype(F32)
    cols = iota((128, 256), 0) == lax.rem(s, 128)
    line = jnp.zeros((1, 128), F32)
    own = jnp.zeros((1, 1), F32)
    for c in range(3):
        velocity = out[c].reshape(128, 128)
        picked = lax.dot_general(velocity, rows, (((0,), (0,)), ((), ())), precision=HIGH,
                                 preferred_element_type=F32)
        snap = jnp.sum(jnp.where(cols, picked, 0.0), axis=0, keepdims=True)
        snap_out[c:c + 1] = snap
        both = lax.dot_general(jnp.broadcast_to(snap, (8, 256)), bt[c], (((1,), (1,)), ((), ())),
                               precision=HIGH, preferred_element_type=F32)
        line = line + both[0:1]
        own = own + jnp.sum(snap * snap, axis=1, keepdims=True)
    line = jnp.where(iota((1, 128), 1) == 127, own, line)
    rowmine[...] = line
    spread(rowmine, rr1, 6, False)
    rr1[me] = line

    settle(r2, 3, GX - 1)
    total = r2[0]
    for i in range(1, GX):
        total = total + r2[i]
    mine[...] = total
    spread(mine, full, 4, False)
    full[me] = total

    settle(rr1, 7, PLANE - 1)
    total = rr1[0]
    for i in range(1, PLANE):
        total = total + rr1[i]
    rowsum[...] = total
    spread(rowsum, rr2, 8, True)
    rr2[gx] = total

    settle(full, 5, PLANE - 1)
    for i in range(PLANE):
        gram_out[4 * i:4 * i + 4] = full[i]
    settle(rr2, 9, GX - 1)
    total = rr2[0]
    for i in range(1, GX):
        total = total + rr2[i]
    row_out[...] = total

    for c in everything:
        c.wait_send()
    settle(r1, 0, PLANE - 1)
    settle(r2, 2, GX - 1)
    settle(full, 4, PLANE - 1)
    settle(rr1, 6, PLANE - 1)
    settle(rr2, 8, GX - 1)


def factorize(a):
    w = (iota((128, 128), 0) == iota((128, 128), 1)).astype(F32)
    both = jnp.concatenate([a, w], axis=1)
    sub = iota((8, 256), 0)
    sub1 = iota((8, 1), 0)
    lane = iota((8, 128), 1)
    ups, invs = [], []
    for b in range(16):
        p = both[8 * b:8 * b + 8]
        diag = jnp.ones((8, 1), F32)
        for j in range(8):
            k = 8 * b + j
            col = p[:, k:k + 1]
            d = col[j:j + 1]
            diag = jnp.where(sub1 == j, d, diag)
            if j < 7:
                pivot = p[j:j + 1] * (1.0 / d)
                p = p - jnp.where(sub > j, col * pivot, 0.0)
        p = p * lax.rsqrt(diag)
        up = jnp.where(lane >= 8 * b + iota((8, 128), 0), p[:, :128], 0.0)
        inv = p[:, 128:]
        ups.append(up)
        invs.append(inv)
        if b < 15:
            both = both - lax.dot_general(up, jnp.concatenate([up, inv], axis=1),
                                          (((0,), (0,)), ((), ())), precision=HIGH,
                                          preferred_element_type=F32)
    return jnp.concatenate(ups, axis=0), jnp.concatenate(invs, axis=0)


def solve_kernel(bt, snap, gram, row, out, factor):
    r = row[...]
    low = jnp.where(iota((128, 128), 0) == 127, r, gram[...])
    full = jnp.where((iota((128, 128), 1) == 127) & (iota((128, 128), 0) < 127), low.T, low)
    upper, inverse = factorize(full * (1.0 / COUNT))
    factor[...] = upper
    last = iota((128, 256), 0) == 127
    for c in range(3):
        stacked = jnp.where(last, snap[c:c + 1], bt[c])
        out[c] = jnp.dot(inverse, stacked, precision=HIGH, preferred_element_type=F32)


def local(flow, basis, sample):
    bt = jnp.pad(jnp.transpose(basis, (1, 0, 2)), ((0, 0), (0, 1), (0, 0)))
    vm = pl.BlockSpec(memory_space=pltpu.VMEM)
    flow_next, snap, gram, row = pl.pallas_call(
        comm_kernel,
        out_shape=[
            jax.ShapeDtypeStruct((4, 8, 16, 128), F32),
            jax.ShapeDtypeStruct((3, 256), F32),
            jax.ShapeDtypeStruct((128, 128), F32),
            jax.ShapeDtypeStruct((1, 128), F32),
        ],
        in_specs=[pl.BlockSpec(memory_space=pl.ANY), vm, vm],
        out_specs=[vm] * 4,
        scratch_shapes=[
            pltpu.VMEM((3, 4, 10, 16, 128), F32),
            pltpu.VMEM((3, 2, 4, 8, 128), F32),
            pltpu.VMEM((3, 8, 128), F32),
            pltpu.VMEM((3, 4, 8, 128), F32),
            pltpu.VMEM((3, 4, 8, 128), F32),
            pltpu.VMEM((3, 8, 128), F32),
            pltpu.VMEM((3, 8, 128), F32),
            pltpu.VMEM((PLANE, 4, 128), F32),
            pltpu.VMEM((PLANE, 4, 128), F32),
            pltpu.VMEM((4, 128), F32),
            pltpu.VMEM((GX, 4, 128), F32),
            pltpu.VMEM((4, 128), F32),
            pltpu.VMEM((PLANE, 4, 128), F32),
            pltpu.VMEM((1, 128), F32),
            pltpu.VMEM((PLANE, 1, 128), F32),
            pltpu.VMEM((1, 128), F32),
            pltpu.VMEM((GX, 1, 128), F32),
            pltpu.SemaphoreType.DMA,
            pltpu.SemaphoreType.DMA((3, 6)),
            pltpu.SemaphoreType.DMA((3, 6)),
            pltpu.SemaphoreType.DMA((10,)),
        ],
        compiler_params=pltpu.CompilerParams(collective_id=0, has_side_effects=True),
    )(flow, bt, sample.reshape(1, 256))
    out, factor = pl.pallas_call(
        solve_kernel,
        out_shape=[
            jax.ShapeDtypeStruct((3, 128, 256), F32),
            jax.ShapeDtypeStruct((128, 128), F32),
        ],
        in_specs=[vm] * 4,
        out_specs=[vm] * 2,
    )(bt, snap, gram, row)
    return (flow_next, jnp.transpose(out, (1, 0, 2)), factor)


def solution(mesh):
    return jax.shard_map(
        local,
        mesh=mesh,
        in_specs=(
            P(None, "gx", "gy", "gz"),
            P(None, None, ("gx", "gy", "gz")),
            P(("gx", "gy", "gz")),
        ),
        out_specs=(P(None, "gx", "gy", "gz"), P(None, None, ("gx", "gy", "gz")), P()),
        check_vma=False,
    )
```

```python
import functools

import jax
import jax.numpy as jnp
from jax import lax
from jax.experimental import pallas as pl
from jax.experimental.pallas import tpu as pltpu
from jax.sharding import PartitionSpec as P

DT_STEP = 0.35
VISCOSITY = 0.2
SOUND_SQ = 1.0
DRIVING = 0.5
GX, GY, GZ = 16, 4, 8
PLANE = GY * GZ
FIRST = 6
COUNT = 3.0 * 256 * GX * GY * GZ
MESH = pl.DeviceIdType.MESH
HIGH = lax.Precision.HIGHEST
F32 = jnp.float32


def iota(shape, dim):
    return lax.broadcasted_iota(jnp.int32, shape, dim)


def stencil(field, flow, out, ylo, yhi, zlo, zhi, ynext, gy, weights):
    lane = iota((16, 128), 1)
    lane8 = iota((8, 128), 1)
    row = iota((16, 128), 0)
    low_z, high_z = zlo[...], zhi[...]

    def body(x, faces):
        zl = pltpu.roll(low_z, 64 - 8 * x, 1)
        zh = pltpu.roll(high_z, lax.rem(128 - 8 * x, 128), 1)
        mid = [field[c, x + 1] for c in range(4)]
        sx, sy, sz, lap = [], [], [], []
        for c in range(4):
            a = mid[c]
            xp, xm = field[c, x + 2], field[c, x]
            above = jnp.where(gy < GY - 1, yhi[c, pl.ds(x, 1), :], 0.0)
            below = jnp.where(gy > 0, ylo[c, pl.ds(x, 1), :], 0.0)
            yp = jnp.where(row == 15, above, pltpu.roll(a, 15, 0))
            ym = jnp.where(row == 0, below, pltpu.roll(a, 1, 0))
            m = 2 * c
            left = jnp.concatenate([zl[:, m:m + 1], zl[:, m + 1:m + 2]], axis=0)
            right = jnp.concatenate([zh[:, m:m + 1], zh[:, m + 1:m + 2]], axis=0)
            zp = jnp.where(lane == 127, right, pltpu.roll(a, 127, 1))
            zm = jnp.where(lane == 0, left, pltpu.roll(a, 1, 1))
            sx.append(0.5 * (xp - xm))
            sy.append(0.5 * (yp - ym))
            sz.append(0.5 * (zp - zm))
            if c < 3:
                lap.append(xp + xm + (yp + ym) + (zp + zm) - 6.0 * a)
        press = (sx[3], sy[3], sz[3])
        for c in range(4):
            if c < 3:
                rate = (VISCOSITY * lap[c] - (mid[0] * sx[c] + mid[1] * sy[c] + mid[2] * sz[c])
                        - press[c])
                if c == 0:
                    rate = rate + DRIVING
            else:
                rate = -SOUND_SQ * (sx[0] + sy[1] + sz[2])
            new = mid[c] + DT_STEP * rate
            if weights is not None:
                new = weights[0] * flow[c, x + 1] + weights[1] * new
            if ynext is None:
                out[c, x] = new
            else:
                out[c, x + 1] = new
                faces = pack(new, c, x, faces, lane8, ynext)
        return faces

    return lax.fori_loop(0, 8, body, jnp.zeros((8, 128), F32))


def pack(new, c, x, faces, lane8, ynext):
    ynext[0, c, pl.ds(x, 1), :] = new[0:1]
    ynext[1, c, pl.ds(x, 1), :] = new[15:16]
    for half in range(2):
        tile = new[8 * half:8 * half + 8]
        spot = 8 * x + 2 * c + half
        faces = jnp.where(lane8 == spot, tile[:, 0:1], faces)
        faces = jnp.where(lane8 == spot + 64, tile[:, 127:128], faces)
    return faces


def comm_kernel(flow, basis, sample, out, snap_out, upper, inverse, row_out,
                bt, both, fields, ysend, zsend, ylo, yhi, zlo, zhi,
                scat, r1, piece, r2, mine, full, rowmine, rr1, rowsum, rr2,
                load_sem, ssem, rsem, gsem):
    gx, gy, gz = (lax.axis_index(n) for n in ("gx", "gy", "gz"))
    me = gy * GZ + gz

    def plane_id(k):
        other = lax.rem(me + k, PLANE)
        return other, (gx, other // GZ, lax.rem(other, GZ))

    def line_id(k):
        return (lax.rem(gx + k, GX), gy, gz)

    load = pltpu.make_async_copy(flow, fields.at[0, :, pl.ds(1, 8)], load_sem.at[0])
    load_bt = pltpu.make_async_copy(basis, bt, load_sem.at[1])
    load_bt.start()
    load.start()
    barrier = pltpu.get_barrier_semaphore()

    def greet_plane(k, carry):
        pl.semaphore_signal(barrier, inc=1, device_id=plane_id(k)[1], device_id_type=MESH)
        return carry

    def greet_line(k, carry):
        pl.semaphore_signal(barrier, inc=1, device_id=line_id(k), device_id_type=MESH)
        return carry

    lax.fori_loop(1, GX, greet_line, 0)
    lax.fori_loop(1, PLANE, greet_plane, 0)

    load_bt.wait()
    gram = jnp.zeros((128, 128), F32)
    blank = jnp.zeros((1, 256), F32)
    for c in range(3):
        block = jnp.concatenate([bt[c], blank], axis=0)
        gram = gram + times_transposed(block, block)
    for i in range(PLANE):
        scat[i] = gram[4 * i:4 * i + 4]

    load.wait()
    lane8 = iota((8, 128), 1)

    def first(x, faces):
        for c in range(4):
            faces = pack(fields[0, c, x + 1], c, x, faces, lane8, ysend.at[0])
        return faces

    zsend[0] = lax.fori_loop(0, 8, first, jnp.zeros((8, 128), F32))
    pl.semaphore_wait(barrier, GX - 1 + PLANE - 1)

    right = {
        "gx": (lax.rem(gx + 1, GX), gy, gz), "gy": (gx, lax.rem(gy + 1, GY), gz),
        "gz": (gx, gy, lax.rem(gz + 1, GZ)),
    }
    left = {
        "gx": (lax.rem(gx + GX - 1, GX), gy, gz), "gy": (gx, lax.rem(gy + GY - 1, GY), gz),
        "gz": (gx, gy, lax.rem(gz + GZ - 1, GZ)),
    }

    def exchange(s):
        f = fields.at[s]
        moves = [
            (f.at[:, pl.ds(1, 1)], f.at[:, pl.ds(9, 1)], left["gx"]),
            (f.at[:, pl.ds(8, 1)], f.at[:, pl.ds(0, 1)], right["gx"]),
            (ysend.at[s, 0], yhi.at[s], left["gy"]),
            (ysend.at[s, 1], ylo.at[s], right["gy"]),
            (zsend.at[s], zhi.at[s], left["gz"]),
            (zsend.at[s], zlo.at[s], right["gz"]),
        ]
        copies = [
            pltpu.make_async_remote_copy(src_ref=a, dst_ref=b, send_sem=ssem.at[s, i],
                                         recv_sem=rsem.at[s, i], device_id=d, device_id_type=MESH)
            for i, (a, b, d) in enumerate(moves)
        ]
        for copy in copies:
            copy.start()
        return copies

    def scatter(k, carry):
        other, where = plane_id(k)
        pltpu.make_async_remote_copy(src_ref=scat.at[other], dst_ref=r1.at[me], send_sem=gsem.at[0],
                                     recv_sem=gsem.at[1], device_id=where, device_id_type=MESH).start()
        return carry

    def spread(src, dst, sems, line):
        def go(k, carry):
            where = line_id(k) if line else plane_id(k)[1]
            pltpu.make_async_remote_copy(src_ref=src, dst_ref=dst.at[gx if line else me],
                                         send_sem=gsem.at[sems], recv_sem=gsem.at[sems + 1],
                                         device_id=where, device_id_type=MESH).start()
            return carry
        lax.fori_loop(1, GX if line else PLANE, go, 0)

    def settle(buf, sem, count):
        part = buf.at[pl.ds(0, count)]
        pltpu.make_async_copy(part, part, gsem.at[sem]).wait()

    def step(s, dst, weights):
        ynext = ysend.at[s + 1] if s < 2 else None
        faces = stencil(fields.at[s], fields.at[0], dst, ylo.at[s], yhi.at[s], zlo.at[s],
                        zhi.at[s], ynext, gy, weights)
        if s < 2:
            zsend[s + 1] = faces

    copies = exchange(0)
    everything = list(copies)
    lax.fori_loop(1, PLANE, scatter, 0)
    r1[me] = scat[me]
    for c in copies:
        c.wait_recv()
    step(0, fields.at[1], None)
    copies = exchange(1)
    everything += copies

    settle(r1, 1, PLANE - 1)
    total = r1[0]
    for i in range(1, PLANE):
        total = total + r1[i]
    piece[...] = total
    spread(piece, r2, 2, True)
    r2[gx] = total

    for c in copies:
        c.wait_recv()
    step(1, fields.at[2], (0.75, 0.25))
    copies = exchange(2)
    everything += copies
    for c in copies:
        c.wait_recv()
    settle(r2, 3, GX - 1)
    total = r2[0]
    for i in range(1, GX):
        total = total + r2[i]
    mine[...] = total
    spread(mine, full, 4, False)
    full[me] = total
    step(2, out, (1.0 / 3.0, 2.0 / 3.0))

    s = sample[...]
    rows = (iota((128, 256), 0) == s // 128).astype(F32)
    cols = iota((128, 256), 0) == lax.rem(s, 128)
    line = jnp.zeros((1, 128), F32)
    for c in range(3):
        velocity = out[c].reshape(128, 128)
        picked = lax.dot_general(velocity, rows, (((0,), (0,)), ((), ())), precision=HIGH,
                                 preferred_element_type=F32)
        snap = jnp.sum(jnp.where(cols, picked, 0.0), axis=0, keepdims=True)
        snap_out[c:c + 1] = snap
        block = jnp.concatenate([bt[c], snap], axis=0)
        line = line + times_transposed(jnp.broadcast_to(snap, (8, 256)), block)[0:1]
    rowmine[...] = line
    spread(rowmine, rr1, 6, False)
    rr1[me] = line

    settle(full, 5, PLANE - 1)
    unit = iota((4, 128), 1)
    for i in range(PLANE):
        below = 4 * i + iota((4, 128), 0)
        corner = (below == 127) & (unit == 127)
        both[4 * i:4 * i + 4, :128] = jnp.where(corner, 1.0, full[i] * (1.0 / COUNT))
        both[4 * i:4 * i + 4, 128:] = (unit == below).astype(F32)
    panel = functools.partial(eliminate, both=both, upper=upper, inverse=inverse)
    lax.fori_loop(0, FIRST, panel, 0)

    settle(rr1, 7, PLANE - 1)
    total = rr1[0]
    for i in range(1, PLANE):
        total = total + rr1[i]
    rowsum[...] = total
    spread(rowsum, rr2, 8, True)
    rr2[gx] = total
    lax.fori_loop(FIRST, 16, panel, 0)
    settle(rr2, 9, GX - 1)
    total = rr2[0]
    for i in range(1, GX):
        total = total + rr2[i]
    row_out[...] = total

    for c in everything:
        c.wait_send()
    settle(r1, 0, PLANE - 1)
    settle(r2, 2, GX - 1)
    settle(full, 4, PLANE - 1)
    settle(rr1, 6, PLANE - 1)
    settle(rr2, 8, GX - 1)


def eliminate(b, carry, both, upper, inverse):
    rows = pl.ds(pl.multiple_of(8 * b, 8), 8)
    p = both[rows, :]
    left, right = p[:, :128], p[:, 128:]
    near = pltpu.roll(left, lax.rem(128 - 8 * b, 128), 1)
    full = (8, 128)
    e = [[None] * 8 for _ in range(8)]
    for k in range(8):
        col = jnp.broadcast_to(near[:, k:k + 1], full)
        for i in range(k, 8):
            e[i][k] = jnp.broadcast_to(col[i:i + 1], full)
    xs = [jnp.broadcast_to(left[i:i + 1], full) for i in range(8)]
    ys = [jnp.broadcast_to(right[i:i + 1], full) for i in range(8)]
    sub = iota(full, 0)
    up, inv = xs[0], ys[0]
    for k in range(8):
        scale = lax.rsqrt(e[k][k])
        up = jnp.where(sub == k, xs[k] * scale, up)
        inv = jnp.where(sub == k, ys[k] * scale, inv)
        if k < 7:
            recip = 1.0 / e[k][k]
            for i in range(k + 1, 8):
                part = e[i][k] * recip
                for m in range(k + 1, i + 1):
                    e[i][m] = e[i][m] - part * e[m][k]
                xs[i] = xs[i] - part * xs[k]
                ys[i] = ys[i] - part * ys[k]
    up = jnp.where(iota(full, 1) >= 8 * b + sub, up, 0.0)
    upper[rows, :] = up
    inverse[rows, :] = inv
    both[...] = both[...] - lax.dot_general(
        up, jnp.concatenate([up, inv], axis=1), (((0,), (0,)), ((), ())), precision=HIGH,
        preferred_element_type=F32)
    return carry


def times_transposed(a, b):
    return lax.dot_general(a, b, (((1,), (1,)), ((), ())), precision=HIGH,
                           preferred_element_type=F32)


def solve_kernel(bt, snap, upper, inverse, row, flow, out, factor, flow_out):
    flow_out[...] = flow[...]
    lane = iota((8, 128), 1)
    w = inverse[...]
    r = jnp.broadcast_to(row[...] * (1.0 / COUNT), (8, 128))
    inner = jnp.where(lane < 127, r, 0.0)
    y = jnp.where(lane < 127, times_transposed(inner, w), 0.0)
    corner = jnp.sum(r - inner, axis=1, keepdims=True) - jnp.sum(y * y, axis=1, keepdims=True)
    scale = lax.rsqrt(corner)
    last = -jnp.dot(y, w, precision=HIGH, preferred_element_type=F32)
    last = jnp.where(lane == 127, 1.0, last) * scale
    w = jnp.where(iota((128, 128), 0) == 127, last[0:1], w)
    edge = jnp.where(lane == 127, corner * scale, y)
    square = jnp.where(iota((128, 128), 1) == 127, jnp.broadcast_to(edge[0:1], (128, 128)).T, upper[...])
    factor[...] = square
    for c in range(3):
        stacked = jnp.concatenate([bt[c], snap[c:c + 1]], axis=0)
        out[c] = jnp.dot(w, stacked, precision=HIGH, preferred_element_type=F32)


def local(flow, basis, sample):
    bt = jnp.transpose(basis, (1, 0, 2))
    vm = pl.BlockSpec(memory_space=pltpu.VMEM)
    hbm = pl.BlockSpec(memory_space=pltpu.HBM)
    square = jax.ShapeDtypeStruct((128, 128), F32)
    whole = jax.ShapeDtypeStruct((4, 8, 16, 128), F32)
    flow_next, snap, upper, inverse, row = pl.pallas_call(
        comm_kernel,
        out_shape=[
            whole,
            jax.ShapeDtypeStruct((3, 256), F32),
            square,
            square,
            jax.ShapeDtypeStruct((1, 128), F32),
        ],
        in_specs=[hbm, hbm, vm],
        out_specs=[vm] * 5,
        scratch_shapes=[
            pltpu.VMEM((3, 127, 256), F32),
            pltpu.VMEM((128, 256), F32),
            pltpu.VMEM((3, 4, 10, 16, 128), F32),
            pltpu.VMEM((3, 2, 4, 8, 128), F32),
            pltpu.VMEM((3, 8, 128), F32),
            pltpu.VMEM((3, 4, 8, 128), F32),
            pltpu.VMEM((3, 4, 8, 128), F32),
            pltpu.VMEM((3, 8, 128), F32),
            pltpu.VMEM((3, 8, 128), F32),
            pltpu.VMEM((PLANE, 4, 128), F32),
            pltpu.VMEM((PLANE, 4, 128), F32),
            pltpu.VMEM((4, 128), F32),
            pltpu.VMEM((GX, 4, 128), F32),
            pltpu.VMEM((4, 128), F32),
            pltpu.VMEM((PLANE, 4, 128), F32),
            pltpu.VMEM((1, 128), F32),
            pltpu.VMEM((PLANE, 1, 128), F32),
            pltpu.VMEM((1, 128), F32),
            pltpu.VMEM((GX, 1, 128), F32),
            pltpu.SemaphoreType.DMA((2,)),
            pltpu.SemaphoreType.DMA((3, 6)),
            pltpu.SemaphoreType.DMA((3, 6)),
            pltpu.SemaphoreType.DMA((10,)),
        ],
        compiler_params=pltpu.CompilerParams(collective_id=0, has_side_effects=True,
                                             vmem_limit_bytes=16 << 20),
    )(flow, bt, sample.reshape(1, 256))
    out, factor, flow_next = pl.pallas_call(
        solve_kernel,
        out_shape=[jax.ShapeDtypeStruct((3, 128, 256), F32), square, whole],
        in_specs=[vm] * 6,
        out_specs=[vm] * 3,
        compiler_params=pltpu.CompilerParams(vmem_limit_bytes=16 << 20),
    )(bt, snap, upper, inverse, row, flow_next)
    return (flow_next, jnp.transpose(out, (1, 0, 2)), factor)


def solution(mesh):
    return jax.shard_map(
        local,
        mesh=mesh,
        in_specs=(
            P(None, "gx", "gy", "gz"),
            P(None, None, ("gx", "gy", "gz")),
            P(("gx", "gy", "gz")),
        ),
        out_specs=(P(None, "gx", "gy", "gz"), P(None, None, ("gx", "gy", "gz")), P()),
        check_vma=False,
    )
```

```python
import functools

import jax
import jax.numpy as jnp
from jax import lax
from jax.experimental import pallas as pl
from jax.experimental.pallas import tpu as pltpu
from jax.sharding import PartitionSpec as P

DT_STEP = 0.35
VISCOSITY = 0.2
SOUND_SQ = 1.0
DRIVING = 0.5
GX, GY, GZ = 16, 4, 8
PLANE = GY * GZ
UNROLL = 4
COUNT = 3.0 * 256 * GX * GY * GZ
MESH = pl.DeviceIdType.MESH
HIGH = lax.Precision.HIGHEST
F32 = jnp.float32


def iota(shape, dim):
    return lax.broadcasted_iota(jnp.int32, shape, dim)


def stencil(field, flow, out, ylo, yhi, zlo, zhi, ynext, gy, weights):
    lane = iota((16, 128), 1)
    lane8 = iota((8, 128), 1)
    row = iota((16, 128), 0)
    low_z, high_z = zlo[...], zhi[...]

    def plane(x, faces):
        zl = pltpu.roll(low_z, 64 - 8 * x, 1)
        zh = pltpu.roll(high_z, lax.rem(128 - 8 * x, 128), 1)
        mid = [field[c, x + 1] for c in range(4)]
        sx, sy, sz, lap = [], [], [], []
        for c in range(4):
            a = mid[c]
            xp, xm = field[c, x + 2], field[c, x]
            above = jnp.where(gy < GY - 1, yhi[c, pl.ds(x, 1), :], 0.0)
            below = jnp.where(gy > 0, ylo[c, pl.ds(x, 1), :], 0.0)
            yp = jnp.where(row == 15, above, pltpu.roll(a, 15, 0))
            ym = jnp.where(row == 0, below, pltpu.roll(a, 1, 0))
            m = 2 * c
            left = jnp.concatenate([zl[:, m:m + 1], zl[:, m + 1:m + 2]], axis=0)
            right = jnp.concatenate([zh[:, m:m + 1], zh[:, m + 1:m + 2]], axis=0)
            zp = jnp.where(lane == 127, right, pltpu.roll(a, 127, 1))
            zm = jnp.where(lane == 0, left, pltpu.roll(a, 1, 1))
            sx.append(0.5 * (xp - xm))
            sy.append(0.5 * (yp - ym))
            sz.append(0.5 * (zp - zm))
            if c < 3:
                lap.append(xp + xm + (yp + ym) + (zp + zm) - 6.0 * a)
        press = (sx[3], sy[3], sz[3])
        for c in range(4):
            if c < 3:
                rate = (VISCOSITY * lap[c] - (mid[0] * sx[c] + mid[1] * sy[c] + mid[2] * sz[c])
                        - press[c])
                if c == 0:
                    rate = rate + DRIVING
            else:
                rate = -SOUND_SQ * (sx[0] + sy[1] + sz[2])
            new = mid[c] + DT_STEP * rate
            if weights is not None:
                new = weights[0] * flow[c, x + 1] + weights[1] * new
            if ynext is None:
                out[c, x] = new
            else:
                out[c, x + 1] = new
                faces = pack(new, c, x, faces, lane8, ynext)
        return faces

    def body(i, faces):
        for d in range(UNROLL):
            faces = plane(UNROLL * i + d, faces)
        return faces

    return lax.fori_loop(0, 8 // UNROLL, body, jnp.zeros((8, 128), F32))


def pack(new, c, x, faces, lane8, ynext):
    ynext[0, c, pl.ds(x, 1), :] = new[0:1]
    ynext[1, c, pl.ds(x, 1), :] = new[15:16]
    for half in range(2):
        tile = new[8 * half:8 * half + 8]
        spot = 8 * x + 2 * c + half
        faces = jnp.where(lane8 == spot, tile[:, 0:1], faces)
        faces = jnp.where(lane8 == spot + 64, tile[:, 127:128], faces)
    return faces


def comm_kernel(flow, basis, sample, out, snap_out, upper_out, inverse_out, row_out,
                bt, both, upper, inverse, snaps, row, fields, ysend, zsend, ylo, yhi, zlo, zhi,
                scat, r1, piece, r2, mine, full, rowmine, rr1, rowsum, rr2,
                load_sem, store_sem, ssem, rsem, gsem, know):
    gx, gy, gz = (lax.axis_index(n) for n in ("gx", "gy", "gz"))
    me = gy * GZ + gz

    def plane_id(k):
        other = lax.rem(me + k, PLANE)
        return other, (gx, other // GZ, lax.rem(other, GZ))

    def at(dx=0, dy=0, dz=0):
        return (lax.rem(gx + dx + GX, GX), lax.rem(gy + dy + GY, GY), lax.rem(gz + dz + GZ, GZ))

    def tell(sem, where):
        pl.semaphore_signal(sem, inc=1, device_id=where, device_id_type=MESH)

    barrier = pltpu.get_barrier_semaphore()
    for d in (1, -1):
        tell(barrier, at(dx=d))
    for d in range(1, GY):
        tell(barrier, at(dy=d))
    for d in range(1, GZ):
        tell(barrier, at(dz=d))
    load = pltpu.make_async_copy(flow, fields.at[0, :, pl.ds(1, 8)], load_sem.at[0])
    load.start()
    load_bt = pltpu.make_async_copy(basis, bt, load_sem.at[1])
    load_bt.start()
    load.wait()
    lane8 = iota((8, 128), 1)

    def first(i, faces):
        for d in range(UNROLL):
            x = UNROLL * i + d
            for c in range(4):
                faces = pack(fields[0, c, x + 1], c, x, faces, lane8, ysend.at[0])
        return faces

    zsend[0] = lax.fori_loop(0, 8 // UNROLL, first, jnp.zeros((8, 128), F32))
    pl.semaphore_wait(barrier, 2 + GY - 1 + GZ - 1)
    for d in range(1, GZ):
        tell(know.at[0], at(dz=d))
    for d in (1, -1):
        tell(know.at[1], at(dx=d))

    def exchange(s):
        f = fields.at[s]
        moves = [
            (f.at[:, pl.ds(1, 1)], f.at[:, pl.ds(9, 1)], at(dx=-1)),
            (f.at[:, pl.ds(8, 1)], f.at[:, pl.ds(0, 1)], at(dx=1)),
            (ysend.at[s, 0], yhi.at[s], at(dy=-1)),
            (ysend.at[s, 1], ylo.at[s], at(dy=1)),
            (zsend.at[s], zhi.at[s], at(dz=-1)),
            (zsend.at[s], zlo.at[s], at(dz=1)),
        ]
        copies = [
            pltpu.make_async_remote_copy(src_ref=a, dst_ref=b, send_sem=ssem.at[s, i],
                                         recv_sem=rsem.at[s, i], device_id=d, device_id_type=MESH)
            for i, (a, b, d) in enumerate(moves)
        ]
        for copy in copies:
            copy.start()
        return copies

    def scatter(k, carry):
        other, where = plane_id(k)
        pltpu.make_async_remote_copy(src_ref=scat.at[other], dst_ref=r1.at[me], send_sem=gsem.at[0],
                                     recv_sem=gsem.at[1], device_id=where, device_id_type=MESH).start()
        return carry

    def spread(src, dst, sems, line):
        def go(k, carry):
            where = at(dx=k) if line else plane_id(k)[1]
            pltpu.make_async_remote_copy(src_ref=src, dst_ref=dst.at[gx if line else me],
                                         send_sem=gsem.at[sems], recv_sem=gsem.at[sems + 1],
                                         device_id=where, device_id_type=MESH).start()
            return carry
        lax.fori_loop(1, GX if line else PLANE, go, 0)

    def settle(buf, sem, count):
        part = buf.at[pl.ds(0, count)]
        pltpu.make_async_copy(part, part, gsem.at[sem]).wait()

    def add_up(buf, count):
        parts = [buf[i] for i in range(count)]
        while len(parts) > 1:
            parts = [a + b for a, b in zip(parts[::2], parts[1::2])]
        return parts[0]

    def step(s, dst, weights):
        ynext = ysend.at[s + 1] if s < 2 else None
        faces = stencil(fields.at[s], fields.at[0], dst, ylo.at[s], yhi.at[s], zlo.at[s],
                        zhi.at[s], ynext, gy, weights)
        if s < 2:
            zsend[s + 1] = faces

    copies = exchange(0)
    everything = list(copies)

    load_bt.wait()
    gram = jnp.zeros((128, 128), F32)
    blank = jnp.zeros((1, 256), F32)
    for c in range(3):
        block = jnp.concatenate([bt[c], blank], axis=0)
        gram = gram + times_transposed(block, block)
    for i in range(PLANE):
        scat[i] = gram[4 * i:4 * i + 4]
    pl.semaphore_wait(know.at[0], GZ - 1)
    lax.fori_loop(1, PLANE, scatter, 0)
    r1[me] = scat[me]
    pl.semaphore_wait(know.at[1], 2)
    for d in (2, -2):
        tell(know.at[2], at(dx=d))

    for c in copies:
        c.wait_recv()
    step(0, fields.at[1], None)
    copies = exchange(1)
    everything += copies

    pl.semaphore_wait(know.at[2], 2)
    for d in (4, -4):
        tell(know.at[3], at(dx=d))
    for c in copies:
        c.wait_recv()
    settle(r1, 1, PLANE - 1)
    pl.semaphore_wait(know.at[3], 2)
    total = add_up(r1, PLANE)
    piece[...] = total
    spread(piece, r2, 2, True)
    r2[gx] = total

    step(1, fields.at[2], (0.75, 0.25))
    copies = exchange(2)
    everything += copies
    for c in copies:
        c.wait_recv()
    result = fields.at[3]
    step(2, result, (1.0 / 3.0, 2.0 / 3.0))
    stores = [pltpu.make_async_copy(result.at[:, pl.ds(0, 8)], out, store_sem.at[0])]
    stores[0].start()

    s = sample[...]
    rows = (iota((128, 256), 0) == s // 128).astype(F32)
    cols = iota((128, 256), 0) == lax.rem(s, 128)
    line = jnp.zeros((1, 128), F32)
    for c in range(3):
        velocity = fields[3, c, 0:8].reshape(128, 128)
        picked = lax.dot_general(velocity, rows, (((0,), (0,)), ((), ())), precision=HIGH,
                                 preferred_element_type=F32)
        snap = jnp.sum(jnp.where(cols, picked, 0.0), axis=0, keepdims=True)
        snaps[c:c + 1] = snap
        block = jnp.concatenate([bt[c], snap], axis=0)
        line = line + times_transposed(jnp.broadcast_to(snap, (8, 256)), block)[0:1]
    rowmine[...] = line
    spread(rowmine, rr1, 6, False)
    rr1[me] = line

    settle(r2, 3, GX - 1)
    total = add_up(r2, GX)
    mine[...] = total
    spread(mine, full, 4, False)
    full[me] = total

    settle(rr1, 7, PLANE - 1)
    total = add_up(rr1, PLANE)
    rowsum[...] = total
    spread(rowsum, rr2, 8, True)
    rr2[gx] = total

    settle(full, 5, PLANE - 1)
    unit = iota((4, 128), 1)
    for i in range(PLANE):
        below = 4 * i + iota((4, 128), 0)
        corner = (below == 127) & (unit == 127)
        both[4 * i:4 * i + 4, :128] = jnp.where(corner, 1.0, full[i] * (1.0 / COUNT))
        both[4 * i:4 * i + 4, 128:] = (unit == below).astype(F32)
    panel = functools.partial(eliminate, both=both, upper=upper, inverse=inverse)
    lax.fori_loop(0, 16, panel, 0)
    for src, dst in ((snaps, snap_out), (upper, upper_out), (inverse, inverse_out)):
        stores.append(pltpu.make_async_copy(src, dst, store_sem.at[len(stores)]))
        stores[-1].start()

    settle(rr2, 9, GX - 1)
    row[...] = add_up(rr2, GX)
    stores.append(pltpu.make_async_copy(row, row_out, store_sem.at[4]))
    stores[-1].start()

    for c in everything:
        c.wait_send()
    settle(r1, 0, PLANE - 1)
    settle(r2, 2, GX - 1)
    settle(full, 4, PLANE - 1)
    settle(rr1, 6, PLANE - 1)
    settle(rr2, 8, GX - 1)
    for c in stores:
        c.wait()


def eliminate(b, carry, both, upper, inverse):
    rows = pl.ds(pl.multiple_of(8 * b, 8), 8)
    p = both[rows, :]
    left, right = p[:, :128], p[:, 128:]
    near = pltpu.roll(left, lax.rem(128 - 8 * b, 128), 1)
    full = (8, 128)
    e = [[None] * 8 for _ in range(8)]
    for k in range(8):
        col = jnp.broadcast_to(near[:, k:k + 1], full)
        for i in range(k, 8):
            e[i][k] = jnp.broadcast_to(col[i:i + 1], full)
    xs = [jnp.broadcast_to(left[i:i + 1], full) for i in range(8)]
    ys = [jnp.broadcast_to(right[i:i + 1], full) for i in range(8)]
    sub = iota(full, 0)
    up, inv = xs[0], ys[0]
    for k in range(8):
        scale = lax.rsqrt(e[k][k])
        up = jnp.where(sub == k, xs[k] * scale, up)
        inv = jnp.where(sub == k, ys[k] * scale, inv)
        if k < 7:
            recip = 1.0 / e[k][k]
            for i in range(k + 1, 8):
                part = e[i][k] * recip
                for m in range(k + 1, i + 1):
                    e[i][m] = e[i][m] - part * e[m][k]
                xs[i] = xs[i] - part * xs[k]
                ys[i] = ys[i] - part * ys[k]
    up = jnp.where(iota(full, 1) >= 8 * b + sub, up, 0.0)
    upper[rows, :] = up
    inverse[rows, :] = inv
    both[...] = both[...] - lax.dot_general(
        up, jnp.concatenate([up, inv], axis=1), (((0,), (0,)), ((), ())), precision=HIGH,
        preferred_element_type=F32)
    return carry


def times_transposed(a, b):
    return lax.dot_general(a, b, (((1,), (1,)), ((), ())), precision=HIGH,
                           preferred_element_type=F32)


def solve_kernel(bt_in, snap_in, upper_in, inverse_in, row_in, flow_in, out_to, factor_to, flow_to,
                 bt, snap, upper, inverse, row, flow, out, factor, sems):
    pairs = ((row_in, row), (inverse_in, inverse), (upper_in, upper), (snap_in, snap),
             (bt_in, bt), (flow_in, flow))
    loads = [pltpu.make_async_copy(a, b, sems.at[i]) for i, (a, b) in enumerate(pairs)]
    for copy in loads:
        copy.start()
    for copy in loads[:4]:
        copy.wait()
    lane = iota((8, 128), 1)
    w = inverse[...]
    r = jnp.broadcast_to(row[...] * (1.0 / COUNT), (8, 128))
    inner = jnp.where(lane < 127, r, 0.0)
    y = jnp.where(lane < 127, times_transposed(inner, w), 0.0)
    corner = jnp.sum(r - inner, axis=1, keepdims=True) - jnp.sum(y * y, axis=1, keepdims=True)
    scale = lax.rsqrt(corner)
    last = -jnp.dot(y, w, precision=HIGH, preferred_element_type=F32)
    last = jnp.where(lane == 127, 1.0, last) * scale
    w = jnp.where(iota((128, 128), 0) == 127, last[0:1], w)
    edge = jnp.where(lane == 127, corner * scale, y)
    square = jnp.where(iota((128, 128), 1) == 127, jnp.broadcast_to(edge[0:1], (128, 128)).T, upper[...])
    factor[...] = square
    stores = []

    def store(a, b):
        stores.append(pltpu.make_async_copy(a, b, sems.at[6 + len(stores)]))
        stores[-1].start()

    store(factor, factor_to)
    for copy in loads[4:]:
        copy.wait()
    store(flow, flow_to)
    for c in range(3):
        stacked = jnp.concatenate([bt[c], snap[c:c + 1]], axis=0)
        out[c] = jnp.dot(w, stacked, precision=HIGH, preferred_element_type=F32)
        store(out.at[c], out_to.at[c])
    for copy in stores:
        copy.wait()


def local(flow, basis, sample):
    bt = jnp.transpose(basis, (1, 0, 2))
    vm = pl.BlockSpec(memory_space=pltpu.VMEM)
    hbm = pl.BlockSpec(memory_space=pltpu.HBM)
    square = jax.ShapeDtypeStruct((128, 128), F32)
    whole = jax.ShapeDtypeStruct((4, 8, 16, 128), F32)
    flow_next, snap, upper, inverse, row = pl.pallas_call(
        comm_kernel,
        out_shape=[
            whole,
            jax.ShapeDtypeStruct((3, 256), F32),
            square,
            square,
            jax.ShapeDtypeStruct((1, 128), F32),
        ],
        in_specs=[hbm, hbm, vm],
        out_specs=[hbm] * 5,
        scratch_shapes=[
            pltpu.VMEM((3, 127, 256), F32),
            pltpu.VMEM((128, 256), F32),
            pltpu.VMEM((128, 128), F32),
            pltpu.VMEM((128, 128), F32),
            pltpu.VMEM((3, 256), F32),
            pltpu.VMEM((1, 128), F32),
            pltpu.VMEM((4, 4, 10, 16, 128), F32),
            pltpu.VMEM((3, 2, 4, 8, 128), F32),
            pltpu.VMEM((3, 8, 128), F32),
            pltpu.VMEM((3, 4, 8, 128), F32),
            pltpu.VMEM((3, 4, 8, 128), F32),
            pltpu.VMEM((3, 8, 128), F32),
            pltpu.VMEM((3, 8, 128), F32),
            pltpu.VMEM((PLANE, 4, 128), F32),
            pltpu.VMEM((PLANE, 4, 128), F32),
            pltpu.VMEM((4, 128), F32),
            pltpu.VMEM((GX, 4, 128), F32),
            pltpu.VMEM((4, 128), F32),
            pltpu.VMEM((PLANE, 4, 128), F32),
            pltpu.VMEM((1, 128), F32),
            pltpu.VMEM((PLANE, 1, 128), F32),
            pltpu.VMEM((1, 128), F32),
            pltpu.VMEM((GX, 1, 128), F32),
            pltpu.SemaphoreType.DMA((2,)),
            pltpu.SemaphoreType.DMA((5,)),
            pltpu.SemaphoreType.DMA((3, 6)),
            pltpu.SemaphoreType.DMA((3, 6)),
            pltpu.SemaphoreType.DMA((10,)),
            pltpu.SemaphoreType.REGULAR((4,)),
        ],
        compiler_params=pltpu.CompilerParams(collective_id=0, has_side_effects=True),
    )(flow, bt, sample.reshape(1, 256))
    out, factor, flow_next = pl.pallas_call(
        solve_kernel,
        out_shape=[jax.ShapeDtypeStruct((3, 128, 256), F32), square, whole],
        in_specs=[hbm] * 6,
        out_specs=[hbm] * 3,
        scratch_shapes=[
            pltpu.VMEM((3, 127, 256), F32),
            pltpu.VMEM((3, 256), F32),
            pltpu.VMEM((128, 128), F32),
            pltpu.VMEM((128, 128), F32),
            pltpu.VMEM((1, 128), F32),
            pltpu.VMEM((4, 8, 16, 128), F32),
            pltpu.VMEM((3, 128, 256), F32),
            pltpu.VMEM((128, 128), F32),
            pltpu.SemaphoreType.DMA((11,)),
        ],
    )(bt, snap, upper, inverse, row, flow_next)
    return (flow_next, jnp.transpose(out, (1, 0, 2)), factor)


def solution(mesh):
    return jax.shard_map(
        local,
        mesh=mesh,
        in_specs=(
            P(None, "gx", "gy", "gz"),
            P(None, None, ("gx", "gy", "gz")),
            P(("gx", "gy", "gz")),
        ),
        out_specs=(P(None, "gx", "gy", "gz"), P(None, None, ("gx", "gy", "gz")), P()),
        check_vma=False,
    )
```

```python
import functools

import jax
import jax.numpy as jnp
from jax import lax
from jax.experimental import pallas as pl
from jax.experimental.pallas import tpu as pltpu
from jax.sharding import PartitionSpec as P

DT_STEP = 0.35
VISCOSITY = 0.2
SOUND_SQ = 1.0
DRIVING = 0.5
GX, GY, GZ = 16, 4, 8
PLANE = GY * GZ
UNROLL = 4
COUNT = 3.0 * 256 * GX * GY * GZ
MESH = pl.DeviceIdType.MESH
HIGH = lax.Precision.HIGHEST
F32 = jnp.float32


def iota(shape, dim):
    return lax.broadcasted_iota(jnp.int32, shape, dim)


def stencil(field, flow, out, ylo, yhi, zlo, zhi, ynext, gy, weights):
    lane = iota((16, 128), 1)
    lane8 = iota((8, 128), 1)
    row = iota((16, 128), 0)
    low_z, high_z = zlo[...], zhi[...]

    def plane(x, faces):
        zl = pltpu.roll(low_z, 64 - 8 * x, 1)
        zh = pltpu.roll(high_z, lax.rem(128 - 8 * x, 128), 1)
        mid = [field[c, x + 1] for c in range(4)]
        sx, sy, sz, lap = [], [], [], []
        for c in range(4):
            a = mid[c]
            xp, xm = field[c, x + 2], field[c, x]
            above = jnp.where(gy < GY - 1, yhi[c, pl.ds(x, 1), :], 0.0)
            below = jnp.where(gy > 0, ylo[c, pl.ds(x, 1), :], 0.0)
            yp = jnp.where(row == 15, above, pltpu.roll(a, 15, 0))
            ym = jnp.where(row == 0, below, pltpu.roll(a, 1, 0))
            m = 2 * c
            left = jnp.concatenate([zl[:, m:m + 1], zl[:, m + 1:m + 2]], axis=0)
            right = jnp.concatenate([zh[:, m:m + 1], zh[:, m + 1:m + 2]], axis=0)
            zp = jnp.where(lane == 127, right, pltpu.roll(a, 127, 1))
            zm = jnp.where(lane == 0, left, pltpu.roll(a, 1, 1))
            sx.append(0.5 * (xp - xm))
            sy.append(0.5 * (yp - ym))
            sz.append(0.5 * (zp - zm))
            if c < 3:
                lap.append(xp + xm + (yp + ym) + (zp + zm) - 6.0 * a)
        press = (sx[3], sy[3], sz[3])
        for c in range(4):
            if c < 3:
                rate = (VISCOSITY * lap[c] - (mid[0] * sx[c] + mid[1] * sy[c] + mid[2] * sz[c])
                        - press[c])
                if c == 0:
                    rate = rate + DRIVING
            else:
                rate = -SOUND_SQ * (sx[0] + sy[1] + sz[2])
            new = mid[c] + DT_STEP * rate
            if weights is not None:
                new = weights[0] * flow[c, x + 1] + weights[1] * new
            if ynext is None:
                out[c, x] = new
            else:
                out[c, x + 1] = new
                faces = pack(new, c, x, faces, lane8, ynext)
        return faces

    def body(i, faces):
        for d in range(UNROLL):
            faces = plane(UNROLL * i + d, faces)
        return faces

    return lax.fori_loop(0, 8 // UNROLL, body, jnp.zeros((8, 128), F32))


def pack(new, c, x, faces, lane8, ynext):
    ynext[0, c, pl.ds(x, 1), :] = new[0:1]
    ynext[1, c, pl.ds(x, 1), :] = new[15:16]
    for half in range(2):
        tile = new[8 * half:8 * half + 8]
        spot = 8 * x + 2 * c + half
        faces = jnp.where(lane8 == spot, tile[:, 0:1], faces)
        faces = jnp.where(lane8 == spot + 64, tile[:, 127:128], faces)
    return faces


def comm_kernel(flow, basis, sample, out, snap_out, upper_out, inverse_out, row_out,
                bt, both, upper, inverse, snaps, row, fields, ysend, zsend, ylo, yhi, zlo, zhi,
                scat, r1, piece, r2, mine, full, rowmine, rr1, rowsum, rr2,
                load_sem, store_sem, ssem, rsem, gsem, know):
    gx, gy, gz = (lax.axis_index(n) for n in ("gx", "gy", "gz"))
    me = gy * GZ + gz

    def plane_id(k):
        other = lax.rem(me + k, PLANE)
        return other, (gx, other // GZ, lax.rem(other, GZ))

    def at(dx=0, dy=0, dz=0):
        return (lax.rem(gx + dx + GX, GX), lax.rem(gy + dy + GY, GY), lax.rem(gz + dz + GZ, GZ))

    def tell(sem, where):
        pl.semaphore_signal(sem, inc=1, device_id=where, device_id_type=MESH)

    barrier = pltpu.get_barrier_semaphore()
    for d in (1, -1):
        tell(barrier, at(dx=d))
    for d in range(1, GY):
        tell(barrier, at(dy=d))
    for d in range(1, GZ):
        tell(barrier, at(dz=d))
    load = pltpu.make_async_copy(flow, fields.at[0, :, pl.ds(1, 8)], load_sem.at[0])
    load.start()
    load_bt = pltpu.make_async_copy(basis, bt, load_sem.at[1])
    load_bt.start()
    load.wait()
    lane8 = iota((8, 128), 1)

    def first(i, faces):
        for d in range(UNROLL):
            x = UNROLL * i + d
            for c in range(4):
                faces = pack(fields[0, c, x + 1], c, x, faces, lane8, ysend.at[0])
        return faces

    zsend[0] = lax.fori_loop(0, 8 // UNROLL, first, jnp.zeros((8, 128), F32))
    pl.semaphore_wait(barrier, 2 + GY - 1 + GZ - 1)
    for d in range(1, GZ):
        tell(know.at[0], at(dz=d))
    for d in (1, -1):
        tell(know.at[1], at(dx=d))

    def exchange(s):
        f = fields.at[s]
        moves = [
            (f.at[:, pl.ds(1, 1)], f.at[:, pl.ds(9, 1)], at(dx=-1)),
            (f.at[:, pl.ds(8, 1)], f.at[:, pl.ds(0, 1)], at(dx=1)),
            (ysend.at[s, 0], yhi.at[s], at(dy=-1)),
            (ysend.at[s, 1], ylo.at[s], at(dy=1)),
            (zsend.at[s], zhi.at[s], at(dz=-1)),
            (zsend.at[s], zlo.at[s], at(dz=1)),
        ]
        copies = [
            pltpu.make_async_remote_copy(src_ref=a, dst_ref=b, send_sem=ssem.at[s, i],
                                         recv_sem=rsem.at[s, i], device_id=d, device_id_type=MESH)
            for i, (a, b, d) in enumerate(moves)
        ]
        for copy in copies:
            copy.start()
        return copies

    def scatter(k, carry):
        other, where = plane_id(k)
        pltpu.make_async_remote_copy(src_ref=scat.at[other], dst_ref=r1.at[me], send_sem=gsem.at[0],
                                     recv_sem=gsem.at[1], device_id=where, device_id_type=MESH).start()
        return carry

    def spread(src, dst, sems, line):
        def go(k, carry):
            where = at(dx=k) if line else plane_id(k)[1]
            pltpu.make_async_remote_copy(src_ref=src, dst_ref=dst.at[gx if line else me],
                                         send_sem=gsem.at[sems], recv_sem=gsem.at[sems + 1],
                                         device_id=where, device_id_type=MESH).start()
            return carry
        lax.fori_loop(1, GX if line else PLANE, go, 0)

    def settle(buf, sem, count):
        part = buf.at[pl.ds(0, count)]
        pltpu.make_async_copy(part, part, gsem.at[sem]).wait()

    def add_up(buf, count):
        parts = [buf[i] for i in range(count)]
        while len(parts) > 1:
            parts = [a + b for a, b in zip(parts[::2], parts[1::2])]
        return parts[0]

    def step(s, dst, weights):
        ynext = ysend.at[s + 1] if s < 2 else None
        faces = stencil(fields.at[s], fields.at[0], dst, ylo.at[s], yhi.at[s], zlo.at[s],
                        zhi.at[s], ynext, gy, weights)
        if s < 2:
            zsend[s + 1] = faces

    copies = exchange(0)
    everything = list(copies)

    load_bt.wait()
    gram = jnp.zeros((128, 128), F32)
    blank = jnp.zeros((1, 256), F32)
    for c in range(3):
        block = jnp.concatenate([bt[c], blank], axis=0)
        gram = gram + times_transposed(block, block)
    for i in range(PLANE):
        scat[i] = gram[4 * i:4 * i + 4]
    pl.semaphore_wait(know.at[0], GZ - 1)
    lax.fori_loop(1, PLANE, scatter, 0)
    r1[me] = scat[me]
    pl.semaphore_wait(know.at[1], 2)
    for d in (2, -2):
        tell(know.at[2], at(dx=d))

    for c in copies:
        c.wait_recv()
    step(0, fields.at[1], None)
    copies = exchange(1)
    everything += copies

    pl.semaphore_wait(know.at[2], 2)
    for d in (4, -4):
        tell(know.at[3], at(dx=d))
    for c in copies:
        c.wait_recv()
    settle(r1, 1, PLANE - 1)
    pl.semaphore_wait(know.at[3], 2)
    total = add_up(r1, PLANE)
    piece[...] = total
    spread(piece, r2, 2, True)
    r2[gx] = total

    step(1, fields.at[2], (0.75, 0.25))
    copies = exchange(2)
    everything += copies
    for c in copies:
        c.wait_recv()
    result = fields.at[3]
    step(2, result, (1.0 / 3.0, 2.0 / 3.0))
    stores = [pltpu.make_async_copy(result.at[:, pl.ds(0, 8)], out, store_sem.at[0])]
    stores[0].start()

    s = sample[...]
    rows = (iota((128, 256), 0) == s // 128).astype(F32)
    cols = iota((128, 256), 0) == lax.rem(s, 128)
    line = jnp.zeros((1, 128), F32)
    for c in range(3):
        velocity = fields[3, c, 0:8].reshape(128, 128)
        picked = lax.dot_general(velocity, rows, (((0,), (0,)), ((), ())), precision=HIGH,
                                 preferred_element_type=F32)
        snap = jnp.sum(jnp.where(cols, picked, 0.0), axis=0, keepdims=True)
        snaps[c:c + 1] = snap
        block = jnp.concatenate([bt[c], snap], axis=0)
        line = line + times_transposed(jnp.broadcast_to(snap, (8, 256)), block)[0:1]
    rowmine[...] = line
    spread(rowmine, rr1, 6, False)
    rr1[me] = line

    settle(r2, 3, GX - 1)
    total = add_up(r2, GX)
    mine[...] = total
    spread(mine, full, 4, False)
    full[me] = total

    settle(rr1, 7, PLANE - 1)
    total = add_up(rr1, PLANE)
    rowsum[...] = total
    spread(rowsum, rr2, 8, True)
    rr2[gx] = total

    settle(full, 5, PLANE - 1)
    unit = iota((4, 128), 1)
    for i in range(PLANE):
        below = 4 * i + iota((4, 128), 0)
        corner = (below == 127) & (unit == 127)
        both[4 * i:4 * i + 4, :128] = jnp.where(corner, 1.0, full[i] * (1.0 / COUNT))
        both[4 * i:4 * i + 4, 128:] = (unit == below).astype(F32)
    panel = functools.partial(eliminate, both=both, upper=upper, inverse=inverse)
    lax.fori_loop(0, 8, panel, 0)
    for src, dst in ((snaps, snap_out), (upper, upper_out), (inverse, inverse_out)):
        stores.append(pltpu.make_async_copy(src, dst, store_sem.at[len(stores)]))
        stores[-1].start()

    settle(rr2, 9, GX - 1)
    row[...] = add_up(rr2, GX)
    stores.append(pltpu.make_async_copy(row, row_out, store_sem.at[4]))
    stores[-1].start()

    for c in everything:
        c.wait_send()
    settle(r1, 0, PLANE - 1)
    settle(r2, 2, GX - 1)
    settle(full, 4, PLANE - 1)
    settle(rr1, 6, PLANE - 1)
    settle(rr2, 8, GX - 1)
    for c in stores:
        c.wait()


def pivots(near, start, left, right, later=None):
    full = (8, 128)
    e = [[None] * 8 for _ in range(8)]
    for k in range(8):
        col = jnp.broadcast_to(near[:, start + k:start + k + 1], full)
        for i in range(k, 8):
            e[i][k] = jnp.broadcast_to(col[i:i + 1], full)
    parts = [left, right]
    if later is not None:
        below = [jnp.broadcast_to(later[0][:, start + k:start + k + 1], full) for k in range(8)]
        parts.append(near)
        lows = [later[1], later[2], later[0]]
    rows = [[jnp.broadcast_to(a[i:i + 1], full) for i in range(8)] for a in parts]
    sub = iota(full, 0)
    up, inv = rows[0][0], rows[1][0]
    for k in range(8):
        scale = lax.rsqrt(e[k][k])
        up = jnp.where(sub == k, rows[0][k] * scale, up)
        inv = jnp.where(sub == k, rows[1][k] * scale, inv)
        if k < 7 or later is not None:
            recip = 1.0 / e[k][k]
        for i in range(k + 1, 8):
            part = e[i][k] * recip
            for m in range(k + 1, i + 1):
                e[i][m] = e[i][m] - part * e[m][k]
            for x in rows:
                x[i] = x[i] - part * x[k]
        if later is not None:
            part = below[k] * recip
            for m in range(k + 1, 8):
                below[m] = below[m] - part * e[m][k]
            lows = [low - part * x[k] for low, x in zip(lows, rows)]
    return (up, inv, lows) if later is not None else (up, inv)


def eliminate(b, carry, both, upper, inverse):
    rows = pl.ds(pl.multiple_of(16 * b, 16), 16) if not isinstance(b, int) else pl.ds(16 * b, 16)
    p = both[rows, :]
    left, right = p[:, :128], p[:, 128:]
    near, start = left, 0
    if isinstance(b, int):
        start = 16 * b
    else:
        near = pltpu.roll(left, lax.rem(128 - 16 * b, 128), 1)
    up_a, inv_a, (left_b, right_b, near_b) = pivots(
        near[:8], start, left[:8], right[:8], (near[8:], left[8:], right[8:]))
    up_b, inv_b = pivots(near_b, start + 8, left_b, right_b)
    up = jnp.concatenate([up_a, up_b], axis=0)
    inv = jnp.concatenate([inv_a, inv_b], axis=0)
    up = jnp.where(iota((16, 128), 1) >= 16 * b + iota((16, 128), 0), up, 0.0)
    upper[rows, :] = up
    inverse[rows, :] = inv
    if not isinstance(b, int) or b < 7:
        both[...] = both[...] - lax.dot_general(
            up, jnp.concatenate([up, inv], axis=1), (((0,), (0,)), ((), ())), precision=HIGH,
            preferred_element_type=F32)
    return carry


def times_transposed(a, b):
    return lax.dot_general(a, b, (((1,), (1,)), ((), ())), precision=HIGH,
                           preferred_element_type=F32)


def solve_kernel(bt_in, snap_in, upper_in, inverse_in, row_in, flow_in, out_to, factor_to, flow_to,
                 bt, snap, upper, inverse, row, flow, out, factor, sems):
    pairs = ((row_in, row), (inverse_in, inverse), (upper_in, upper), (snap_in, snap),
             (bt_in, bt), (flow_in, flow))
    loads = [pltpu.make_async_copy(a, b, sems.at[i]) for i, (a, b) in enumerate(pairs)]
    for copy in loads:
        copy.start()
    for copy in loads[:4]:
        copy.wait()
    lane = iota((8, 128), 1)
    w = inverse[...]
    r = jnp.broadcast_to(row[...] * (1.0 / COUNT), (8, 128))
    inner = jnp.where(lane < 127, r, 0.0)
    y = jnp.where(lane < 127, times_transposed(inner, w), 0.0)
    corner = jnp.sum(r - inner, axis=1, keepdims=True) - jnp.sum(y * y, axis=1, keepdims=True)
    scale = lax.rsqrt(corner)
    last = -jnp.dot(y, w, precision=HIGH, preferred_element_type=F32)
    last = jnp.where(lane == 127, 1.0, last) * scale
    w = jnp.where(iota((128, 128), 0) == 127, last[0:1], w)
    edge = jnp.where(lane == 127, corner * scale, y)
    square = jnp.where(iota((128, 128), 1) == 127, jnp.broadcast_to(edge[0:1], (128, 128)).T, upper[...])
    factor[...] = square
    stores = []

    def store(a, b):
        stores.append(pltpu.make_async_copy(a, b, sems.at[6 + len(stores)]))
        stores[-1].start()

    store(factor, factor_to)
    for copy in loads[4:]:
        copy.wait()
    store(flow, flow_to)
    for c in range(3):
        stacked = jnp.concatenate([bt[c], snap[c:c + 1]], axis=0)
        out[c] = jnp.dot(w, stacked, precision=HIGH, preferred_element_type=F32)
        store(out.at[c], out_to.at[c])
    for copy in stores:
        copy.wait()


def local(flow, basis, sample):
    bt = jnp.transpose(basis, (1, 0, 2))
    vm = pl.BlockSpec(memory_space=pltpu.VMEM)
    hbm = pl.BlockSpec(memory_space=pltpu.HBM)
    square = jax.ShapeDtypeStruct((128, 128), F32)
    whole = jax.ShapeDtypeStruct((4, 8, 16, 128), F32)
    flow_next, snap, upper, inverse, row = pl.pallas_call(
        comm_kernel,
        out_shape=[
            whole,
            jax.ShapeDtypeStruct((3, 256), F32),
            square,
            square,
            jax.ShapeDtypeStruct((1, 128), F32),
        ],
        in_specs=[hbm, hbm, vm],
        out_specs=[hbm] * 5,
        scratch_shapes=[
            pltpu.VMEM((3, 127, 256), F32),
            pltpu.VMEM((128, 256), F32),
            pltpu.VMEM((128, 128), F32),
            pltpu.VMEM((128, 128), F32),
            pltpu.VMEM((3, 256), F32),
            pltpu.VMEM((1, 128), F32),
            pltpu.VMEM((4, 4, 10, 16, 128), F32),
            pltpu.VMEM((3, 2, 4, 8, 128), F32),
            pltpu.VMEM((3, 8, 128), F32),
            pltpu.VMEM((3, 4, 8, 128), F32),
            pltpu.VMEM((3, 4, 8, 128), F32),
            pltpu.VMEM((3, 8, 128), F32),
            pltpu.VMEM((3, 8, 128), F32),
            pltpu.VMEM((PLANE, 4, 128), F32),
            pltpu.VMEM((PLANE, 4, 128), F32),
            pltpu.VMEM((4, 128), F32),
            pltpu.VMEM((GX, 4, 128), F32),
            pltpu.VMEM((4, 128), F32),
            pltpu.VMEM((PLANE, 4, 128), F32),
            pltpu.VMEM((1, 128), F32),
            pltpu.VMEM((PLANE, 1, 128), F32),
            pltpu.VMEM((1, 128), F32),
            pltpu.VMEM((GX, 1, 128), F32),
            pltpu.SemaphoreType.DMA((2,)),
            pltpu.SemaphoreType.DMA((5,)),
            pltpu.SemaphoreType.DMA((3, 6)),
            pltpu.SemaphoreType.DMA((3, 6)),
            pltpu.SemaphoreType.DMA((10,)),
            pltpu.SemaphoreType.REGULAR((4,)),
        ],
        compiler_params=pltpu.CompilerParams(collective_id=0, has_side_effects=True),
    )(flow, bt, sample.reshape(1, 256))
    out, factor, flow_next = pl.pallas_call(
        solve_kernel,
        out_shape=[jax.ShapeDtypeStruct((3, 128, 256), F32), square, whole],
        in_specs=[hbm] * 6,
        out_specs=[hbm] * 3,
        scratch_shapes=[
            pltpu.VMEM((3, 127, 256), F32),
            pltpu.VMEM((3, 256), F32),
            pltpu.VMEM((128, 128), F32),
            pltpu.VMEM((128, 128), F32),
            pltpu.VMEM((1, 128), F32),
            pltpu.VMEM((4, 8, 16, 128), F32),
            pltpu.VMEM((3, 128, 256), F32),
            pltpu.VMEM((128, 128), F32),
            pltpu.SemaphoreType.DMA((11,)),
        ],
    )(bt, snap, upper, inverse, row, flow_next)
    return (flow_next, jnp.transpose(out, (1, 0, 2)), factor)


def solution(mesh):
    return jax.shard_map(
        local,
        mesh=mesh,
        in_specs=(
            P(None, "gx", "gy", "gz"),
            P(None, None, ("gx", "gy", "gz")),
            P(("gx", "gy", "gz")),
        ),
        out_specs=(P(None, "gx", "gy", "gz"), P(None, None, ("gx", "gy", "gz")), P()),
        check_vma=False,
    )
```

```python
import functools

import jax
import jax.numpy as jnp
from jax import lax
from jax.experimental import pallas as pl
from jax.experimental.pallas import tpu as pltpu
from jax.sharding import PartitionSpec as P

DT_STEP = 0.35
VISCOSITY = 0.2
SOUND_SQ = 1.0
DRIVING = 0.5
GX, GY, GZ = 16, 4, 8
PLANE = GY * GZ
UNROLL = 4
COUNT = 3.0 * 256 * GX * GY * GZ
MESH = pl.DeviceIdType.MESH
HIGH = lax.Precision.HIGHEST
F32 = jnp.float32


def iota(shape, dim):
    return lax.broadcasted_iota(jnp.int32, shape, dim)


def stencil(field, flow, out, ylo, yhi, zlo, zhi, ynext, gy, weights, early):
    lane = iota((16, 128), 1)
    lane8 = iota((8, 128), 1)
    row = iota((16, 128), 0)
    low_z, high_z = zlo[...], zhi[...]

    def plane(x, faces):
        zl = pltpu.roll(low_z, 64 - 8 * x, 1)
        zh = pltpu.roll(high_z, (128 - 8 * x) % 128, 1)
        mid = [field[c, x + 1] for c in range(4)]
        sx, sy, sz, lap = [], [], [], []
        for c in range(4):
            a = mid[c]
            xp, xm = field[c, x + 2], field[c, x]
            above = jnp.where(gy < GY - 1, yhi[c, pl.ds(x, 1), :], 0.0)
            below = jnp.where(gy > 0, ylo[c, pl.ds(x, 1), :], 0.0)
            yp = jnp.where(row == 15, above, pltpu.roll(a, 15, 0))
            ym = jnp.where(row == 0, below, pltpu.roll(a, 1, 0))
            m = 2 * c
            left = jnp.concatenate([zl[:, m:m + 1], zl[:, m + 1:m + 2]], axis=0)
            right = jnp.concatenate([zh[:, m:m + 1], zh[:, m + 1:m + 2]], axis=0)
            zp = jnp.where(lane == 127, right, pltpu.roll(a, 127, 1))
            zm = jnp.where(lane == 0, left, pltpu.roll(a, 1, 1))
            sx.append(0.5 * (xp - xm))
            sy.append(0.5 * (yp - ym))
            sz.append(0.5 * (zp - zm))
            if c < 3:
                lap.append(xp + xm + (yp + ym) + (zp + zm) - 6.0 * a)
        press = (sx[3], sy[3], sz[3])
        for c in range(4):
            if c < 3:
                rate = (VISCOSITY * lap[c] - (mid[0] * sx[c] + mid[1] * sy[c] + mid[2] * sz[c])
                        - press[c])
                if c == 0:
                    rate = rate + DRIVING
            else:
                rate = -SOUND_SQ * (sx[0] + sy[1] + sz[2])
            new = mid[c] + DT_STEP * rate
            if weights is not None:
                new = weights[0] * flow[c, x + 1] + weights[1] * new
            if ynext is None:
                out[c, x] = new
            else:
                out[c, x + 1] = new
                faces = pack(new, c, x, faces, lane8, ynext)
        return faces

    def body(i, faces):
        for x in (3 * i, 7 - 3 * i, 1 + 4 * i, 2 + 4 * i):
            faces = plane(x, faces)
        if early is not None:
            pl.when(i == 0)(early)
        return faces

    return lax.fori_loop(0, 2, body, jnp.zeros((8, 128), F32))


def pack(new, c, x, faces, lane8, ynext):
    ynext[0, c, pl.ds(x, 1), :] = new[0:1]
    ynext[1, c, pl.ds(x, 1), :] = new[15:16]
    for half in range(2):
        tile = new[8 * half:8 * half + 8]
        spot = 8 * x + 2 * c + half
        faces = jnp.where(lane8 == spot, tile[:, 0:1], faces)
        faces = jnp.where(lane8 == spot + 64, tile[:, 127:128], faces)
    return faces


def comm_kernel(flow, basis, sample_in, out, snap_out, upper_out, inverse_out, row_out,
                sample, bt, both, upper, inverse, snaps, row, fields, ysend, zsend, ylo, yhi, zlo, zhi,
                scat, r1, piece, r2, mine, full, rowmine, rr1, rowsum, rr2,
                load_sem, store_sem, ssem, rsem, gsem, know):
    gx, gy, gz = (lax.axis_index(n) for n in ("gx", "gy", "gz"))
    me = gy * GZ + gz

    def plane_id(k):
        other = lax.rem(me + k, PLANE)
        return other, (gx, other // GZ, lax.rem(other, GZ))

    def at(dx=0, dy=0, dz=0):
        return (lax.rem(gx + dx + GX, GX), lax.rem(gy + dy + GY, GY), lax.rem(gz + dz + GZ, GZ))

    def tell(sem, where):
        pl.semaphore_signal(sem, inc=1, device_id=where, device_id_type=MESH)

    barrier = pltpu.get_barrier_semaphore()
    for d in (1, -1):
        tell(barrier, at(dx=d))
    for d in range(1, GY):
        tell(barrier, at(dy=d))
    for d in range(1, GZ):
        tell(barrier, at(dz=d))
    load = pltpu.make_async_copy(flow, fields.at[0, :, pl.ds(1, 8)], load_sem.at[0])
    load.start()
    load_bt = pltpu.make_async_copy(basis, bt, load_sem.at[1])
    load_bt.start()
    load_sample = pltpu.make_async_copy(sample_in, sample, load_sem.at[2])
    load_sample.start()
    load.wait()
    lane8 = iota((8, 128), 1)

    def first(i, faces):
        for d in range(UNROLL):
            x = UNROLL * i + d
            for c in range(4):
                faces = pack(fields[0, c, x + 1], c, x, faces, lane8, ysend.at[0])
        return faces

    zsend[0] = lax.fori_loop(0, 8 // UNROLL, first, jnp.zeros((8, 128), F32))
    pl.semaphore_wait(barrier, 2 + GY - 1 + GZ - 1)
    for d in range(1, GZ):
        tell(know.at[0], at(dz=d))
    for d in (1, -1):
        tell(know.at[1], at(dx=d))

    def moves(s, which=range(6)):
        f = fields.at[s]
        ends = [
            (f.at[:, pl.ds(1, 1)], f.at[:, pl.ds(9, 1)], at(dx=-1)),
            (f.at[:, pl.ds(8, 1)], f.at[:, pl.ds(0, 1)], at(dx=1)),
            (ysend.at[s, 0], yhi.at[s], at(dy=-1)),
            (ysend.at[s, 1], ylo.at[s], at(dy=1)),
            (zsend.at[s], zhi.at[s], at(dz=-1)),
            (zsend.at[s], zlo.at[s], at(dz=1)),
        ]
        return [
            pltpu.make_async_remote_copy(src_ref=ends[i][0], dst_ref=ends[i][1],
                                         send_sem=ssem.at[s, i], recv_sem=rsem.at[s, i],
                                         device_id=ends[i][2], device_id_type=MESH)
            for i in which
        ]

    def exchange(s, which):
        for copy in moves(s, which):
            copy.start()

    def scatter(k, carry):
        other, where = plane_id(k)
        pltpu.make_async_remote_copy(src_ref=scat.at[other], dst_ref=r1.at[me], send_sem=gsem.at[0],
                                     recv_sem=gsem.at[1], device_id=where, device_id_type=MESH).start()
        return carry

    def spread(src, dst, sems, line):
        def go(k, carry):
            where = at(dx=k) if line else plane_id(k)[1]
            pltpu.make_async_remote_copy(src_ref=src, dst_ref=dst.at[gx if line else me],
                                         send_sem=gsem.at[sems], recv_sem=gsem.at[sems + 1],
                                         device_id=where, device_id_type=MESH).start()
            return carry
        lax.fori_loop(1, GX if line else PLANE, go, 0)

    def settle(buf, sem, count):
        part = buf.at[pl.ds(0, count)]
        pltpu.make_async_copy(part, part, gsem.at[sem]).wait()

    def add_up(buf, count):
        parts = [buf[i] for i in range(count)]
        while len(parts) > 1:
            parts = [a + b for a, b in zip(parts[::2], parts[1::2])]
        return parts[0]

    def step(s, dst, weights):
        ynext = ysend.at[s + 1] if s < 2 else None
        early = functools.partial(exchange, s + 1, range(2)) if s < 2 else None
        faces = stencil(fields.at[s], fields.at[0], dst, ylo.at[s], yhi.at[s], zlo.at[s],
                        zhi.at[s], ynext, gy, weights, early)
        if s < 2:
            zsend[s + 1] = faces
            exchange(s + 1, range(2, 6))

    exchange(0, range(6))

    load_bt.wait()
    gram = jnp.zeros((128, 128), F32)
    blank = jnp.zeros((1, 256), F32)
    for c in range(3):
        block = jnp.concatenate([bt[c], blank], axis=0)
        gram = gram + times_transposed(block, block)
    for i in range(PLANE):
        scat[i] = gram[4 * i:4 * i + 4]
    pl.semaphore_wait(know.at[0], GZ - 1)
    lax.fori_loop(1, PLANE, scatter, 0)
    r1[me] = scat[me]
    pl.semaphore_wait(know.at[1], 2)
    for d in (2, -2):
        tell(know.at[2], at(dx=d))

    for c in moves(0):
        c.wait_recv()
    step(0, fields.at[1], None)

    pl.semaphore_wait(know.at[2], 2)
    for d in (4, -4):
        tell(know.at[3], at(dx=d))
    for c in moves(1):
        c.wait_recv()
    settle(r1, 1, PLANE - 1)
    pl.semaphore_wait(know.at[3], 2)
    total = add_up(r1, PLANE)
    piece[...] = total
    spread(piece, r2, 2, True)
    r2[gx] = total

    step(1, fields.at[2], (0.75, 0.25))
    for c in moves(2):
        c.wait_recv()
    result = fields.at[3]
    step(2, result, (1.0 / 3.0, 2.0 / 3.0))
    stores = [pltpu.make_async_copy(result.at[:, pl.ds(0, 8)], out, store_sem.at[0])]
    stores[0].start()

    load_sample.wait()
    s = sample[...]
    rows = (iota((128, 256), 0) == s // 128).astype(F32)
    cols = iota((128, 256), 0) == lax.rem(s, 128)
    line = jnp.zeros((1, 128), F32)
    for c in range(3):
        velocity = fields[3, c, 0:8].reshape(128, 128)
        picked = lax.dot_general(velocity, rows, (((0,), (0,)), ((), ())), precision=HIGH,
                                 preferred_element_type=F32)
        snap = jnp.sum(jnp.where(cols, picked, 0.0), axis=0, keepdims=True)
        snaps[c:c + 1] = snap
        block = jnp.concatenate([bt[c], snap], axis=0)
        line = line + times_transposed(jnp.broadcast_to(snap, (8, 256)), block)[0:1]
    rowmine[...] = line
    spread(rowmine, rr1, 6, False)
    rr1[me] = line

    settle(r2, 3, GX - 1)
    total = add_up(r2, GX)
    mine[...] = total
    spread(mine, full, 4, False)
    full[me] = total

    settle(rr1, 7, PLANE - 1)
    total = add_up(rr1, PLANE)
    rowsum[...] = total
    spread(rowsum, rr2, 8, True)
    rr2[gx] = total

    settle(full, 5, PLANE - 1)
    unit = iota((4, 128), 1)
    for i in range(PLANE):
        below = 4 * i + iota((4, 128), 0)
        corner = (below == 127) & (unit == 127)
        both[4 * i:4 * i + 4, :128] = jnp.where(corner, 1.0, full[i] * (1.0 / COUNT))
        both[4 * i:4 * i + 4, 128:] = (unit == below).astype(F32)
    panel = functools.partial(eliminate, both=both, upper=upper, inverse=inverse)
    lax.fori_loop(0, 8, panel, 0)
    for src, dst in ((snaps, snap_out), (upper, upper_out), (inverse, inverse_out)):
        stores.append(pltpu.make_async_copy(src, dst, store_sem.at[len(stores)]))
        stores[-1].start()

    settle(rr2, 9, GX - 1)
    row[...] = add_up(rr2, GX)
    stores.append(pltpu.make_async_copy(row, row_out, store_sem.at[4]))
    stores[-1].start()

    for s in range(3):
        for c in moves(s):
            c.wait_send()
    settle(r1, 0, PLANE - 1)
    settle(r2, 2, GX - 1)
    settle(full, 4, PLANE - 1)
    settle(rr1, 6, PLANE - 1)
    settle(rr2, 8, GX - 1)
    for c in stores:
        c.wait()


def pivots(near, start, left, right, later=None):
    full = (8, 128)
    e = [[None] * 8 for _ in range(8)]
    for k in range(8):
        col = jnp.broadcast_to(near[:, start + k:start + k + 1], full)
        for i in range(k, 8):
            e[i][k] = jnp.broadcast_to(col[i:i + 1], full)
    parts = [left, right]
    if later is not None:
        below = [jnp.broadcast_to(later[0][:, start + k:start + k + 1], full) for k in range(8)]
        parts.append(near)
        lows = [later[1], later[2], later[0]]
    rows = [[jnp.broadcast_to(a[i:i + 1], full) for i in range(8)] for a in parts]
    sub = iota(full, 0)
    up, inv = rows[0][0], rows[1][0]
    for k in range(8):
        scale = lax.rsqrt(e[k][k])
        up = jnp.where(sub == k, rows[0][k] * scale, up)
        inv = jnp.where(sub == k, rows[1][k] * scale, inv)
        if k < 7 or later is not None:
            recip = 1.0 / e[k][k]
        for i in range(k + 1, 8):
            part = e[i][k] * recip
            for m in range(k + 1, i + 1):
                e[i][m] = e[i][m] - part * e[m][k]
            for x in rows:
                x[i] = x[i] - part * x[k]
        if later is not None:
            part = below[k] * recip
            for m in range(k + 1, 8):
                below[m] = below[m] - part * e[m][k]
            lows = [low - part * x[k] for low, x in zip(lows, rows)]
    return (up, inv, lows) if later is not None else (up, inv)


def eliminate(b, carry, both, upper, inverse):
    rows = pl.ds(pl.multiple_of(16 * b, 16), 16) if not isinstance(b, int) else pl.ds(16 * b, 16)
    p = both[rows, :]
    left, right = p[:, :128], p[:, 128:]
    near, start = left, 0
    if isinstance(b, int):
        start = 16 * b
    else:
        near = pltpu.roll(left, lax.rem(128 - 16 * b, 128), 1)
    up_a, inv_a, (left_b, right_b, near_b) = pivots(
        near[:8], start, left[:8], right[:8], (near[8:], left[8:], right[8:]))
    up_b, inv_b = pivots(near_b, start + 8, left_b, right_b)
    up = jnp.concatenate([up_a, up_b], axis=0)
    inv = jnp.concatenate([inv_a, inv_b], axis=0)
    up = jnp.where(iota((16, 128), 1) >= 16 * b + iota((16, 128), 0), up, 0.0)
    upper[rows, :] = up
    inverse[rows, :] = inv
    if not isinstance(b, int) or b < 7:
        both[...] = both[...] - lax.dot_general(
            up, jnp.concatenate([up, inv], axis=1), (((0,), (0,)), ((), ())), precision=HIGH,
            preferred_element_type=F32)
    return carry


def times_transposed(a, b):
    return lax.dot_general(a, b, (((1,), (1,)), ((), ())), precision=HIGH,
                           preferred_element_type=F32)


def solve_kernel(bt_in, snap_in, upper_in, inverse_in, row_in, flow_in, out_to, factor_to, flow_to,
                 bt, snap, upper, inverse, row, flow, out, factor, sems):
    pairs = ((row_in, row), (inverse_in, inverse), (upper_in, upper), (snap_in, snap),
             (bt_in, bt), (flow_in, flow))
    loads = [pltpu.make_async_copy(a, b, sems.at[i]) for i, (a, b) in enumerate(pairs)]
    for copy in loads:
        copy.start()
    for copy in loads[:4]:
        copy.wait()
    lane = iota((8, 128), 1)
    w = inverse[...]
    r = jnp.broadcast_to(row[...] * (1.0 / COUNT), (8, 128))
    inner = jnp.where(lane < 127, r, 0.0)
    y = jnp.where(lane < 127, times_transposed(inner, w), 0.0)
    corner = jnp.sum(r - inner, axis=1, keepdims=True) - jnp.sum(y * y, axis=1, keepdims=True)
    scale = lax.rsqrt(corner)
    last = -jnp.dot(y, w, precision=HIGH, preferred_element_type=F32)
    last = jnp.where(lane == 127, 1.0, last) * scale
    w = jnp.where(iota((128, 128), 0) == 127, last[0:1], w)
    edge = jnp.where(lane == 127, corner * scale, y)
    square = jnp.where(iota((128, 128), 1) == 127, jnp.broadcast_to(edge[0:1], (128, 128)).T, upper[...])
    factor[...] = square
    stores = []

    def store(a, b):
        stores.append(pltpu.make_async_copy(a, b, sems.at[6 + len(stores)]))
        stores[-1].start()

    store(factor, factor_to)
    for copy in loads[4:]:
        copy.wait()
    store(flow, flow_to)
    for c in range(3):
        stacked = jnp.concatenate([bt[c], snap[c:c + 1]], axis=0)
        out[c] = jnp.dot(w, stacked, precision=HIGH, preferred_element_type=F32)
        store(out.at[c], out_to.at[c])
    for copy in stores:
        copy.wait()


def local(flow, basis, sample):
    bt = jnp.transpose(basis, (1, 0, 2))
    hbm = pl.BlockSpec(memory_space=pltpu.HBM)
    square = jax.ShapeDtypeStruct((128, 128), F32)
    whole = jax.ShapeDtypeStruct((4, 8, 16, 128), F32)
    flow_next, snap, upper, inverse, row = pl.pallas_call(
        comm_kernel,
        out_shape=[
            whole,
            jax.ShapeDtypeStruct((3, 256), F32),
            square,
            square,
            jax.ShapeDtypeStruct((1, 128), F32),
        ],
        in_specs=[hbm, hbm, hbm],
        out_specs=[hbm] * 5,
        scratch_shapes=[
            pltpu.VMEM((1, 256), jnp.int32),
            pltpu.VMEM((3, 127, 256), F32),
            pltpu.VMEM((128, 256), F32),
            pltpu.VMEM((128, 128), F32),
            pltpu.VMEM((128, 128), F32),
            pltpu.VMEM((3, 256), F32),
            pltpu.VMEM((1, 128), F32),
            pltpu.VMEM((4, 4, 10, 16, 128), F32),
            pltpu.VMEM((3, 2, 4, 8, 128), F32),
            pltpu.VMEM((3, 8, 128), F32),
            pltpu.VMEM((3, 4, 8, 128), F32),
            pltpu.VMEM((3, 4, 8, 128), F32),
            pltpu.VMEM((3, 8, 128), F32),
            pltpu.VMEM((3, 8, 128), F32),
            pltpu.VMEM((PLANE, 4, 128), F32),
            pltpu.VMEM((PLANE, 4, 128), F32),
            pltpu.VMEM((4, 128), F32),
            pltpu.VMEM((GX, 4, 128), F32),
            pltpu.VMEM((4, 128), F32),
            pltpu.VMEM((PLANE, 4, 128), F32),
            pltpu.VMEM((1, 128), F32),
            pltpu.VMEM((PLANE, 1, 128), F32),
            pltpu.VMEM((1, 128), F32),
            pltpu.VMEM((GX, 1, 128), F32),
            pltpu.SemaphoreType.DMA((3,)),
            pltpu.SemaphoreType.DMA((5,)),
            pltpu.SemaphoreType.DMA((3, 6)),
            pltpu.SemaphoreType.DMA((3, 6)),
            pltpu.SemaphoreType.DMA((10,)),
            pltpu.SemaphoreType.REGULAR((4,)),
        ],
        compiler_params=pltpu.CompilerParams(collective_id=0, has_side_effects=True,
                                             vmem_limit_bytes=56000000),
    )(flow, bt, sample.reshape(1, 256))
    out, factor, flow_next = pl.pallas_call(
        solve_kernel,
        out_shape=[jax.ShapeDtypeStruct((3, 128, 256), F32), square, whole],
        in_specs=[hbm] * 6,
        out_specs=[hbm] * 3,
        scratch_shapes=[
            pltpu.VMEM((3, 127, 256), F32),
            pltpu.VMEM((3, 256), F32),
            pltpu.VMEM((128, 128), F32),
            pltpu.VMEM((128, 128), F32),
            pltpu.VMEM((1, 128), F32),
            pltpu.VMEM((4, 8, 16, 128), F32),
            pltpu.VMEM((3, 128, 256), F32),
            pltpu.VMEM((128, 128), F32),
            pltpu.SemaphoreType.DMA((11,)),
        ],
        compiler_params=pltpu.CompilerParams(vmem_limit_bytes=16 << 20),
    )(bt, snap, upper, inverse, row, flow_next)
    return (flow_next, jnp.transpose(out, (1, 0, 2)), factor)


def solution(mesh):
    return jax.shard_map(
        local,
        mesh=mesh,
        in_specs=(
            P(None, "gx", "gy", "gz"),
            P(None, None, ("gx", "gy", "gz")),
            P(("gx", "gy", "gz")),
        ),
        out_specs=(P(None, "gx", "gy", "gz"), P(None, None, ("gx", "gy", "gz")), P()),
        check_vma=False,
    )
```

```python
import functools

import jax
import jax.numpy as jnp
from jax import lax
from jax.experimental import pallas as pl
from jax.experimental.pallas import tpu as pltpu
from jax.sharding import PartitionSpec as P

DT_STEP = 0.35
VISCOSITY = 0.2
SOUND_SQ = 1.0
DRIVING = 0.5
GX, GY, GZ = 16, 4, 8
PLANE = GY * GZ
UNROLL = 4
COUNT = 3.0 * 256 * GX * GY * GZ
MESH = pl.DeviceIdType.MESH
HIGH = lax.Precision.HIGHEST
F32 = jnp.float32


def iota(shape, dim):
    return lax.broadcasted_iota(jnp.int32, shape, dim)


def stencil(field, flow, out, ylo, yhi, zlo, zhi, ynext, gy, weights, early):
    lane = iota((16, 128), 1)
    lane8 = iota((8, 128), 1)
    row = iota((16, 128), 0)
    low_z, high_z = zlo[...], zhi[...]

    def plane(x, faces):
        zl = pltpu.roll(low_z, 64 - 8 * x, 1)
        zh = pltpu.roll(high_z, (128 - 8 * x) % 128, 1)
        mid = [field[c, x + 1] for c in range(4)]
        sx, sy, sz, lap = [], [], [], []
        for c in range(4):
            a = mid[c]
            xp, xm = field[c, x + 2], field[c, x]
            above = jnp.where(gy < GY - 1, yhi[c, pl.ds(x, 1), :], 0.0)
            below = jnp.where(gy > 0, ylo[c, pl.ds(x, 1), :], 0.0)
            yp = jnp.where(row == 15, above, pltpu.roll(a, 15, 0))
            ym = jnp.where(row == 0, below, pltpu.roll(a, 1, 0))
            m = 2 * c
            left = jnp.concatenate([zl[:, m:m + 1], zl[:, m + 1:m + 2]], axis=0)
            right = jnp.concatenate([zh[:, m:m + 1], zh[:, m + 1:m + 2]], axis=0)
            zp = jnp.where(lane == 127, right, pltpu.roll(a, 127, 1))
            zm = jnp.where(lane == 0, left, pltpu.roll(a, 1, 1))
            sx.append(0.5 * (xp - xm))
            sy.append(0.5 * (yp - ym))
            sz.append(0.5 * (zp - zm))
            if c < 3:
                lap.append(xp + xm + (yp + ym) + (zp + zm) - 6.0 * a)
        press = (sx[3], sy[3], sz[3])
        for c in range(4):
            if c < 3:
                rate = (VISCOSITY * lap[c] - (mid[0] * sx[c] + mid[1] * sy[c] + mid[2] * sz[c])
                        - press[c])
                if c == 0:
                    rate = rate + DRIVING
            else:
                rate = -SOUND_SQ * (sx[0] + sy[1] + sz[2])
            new = mid[c] + DT_STEP * rate
            if weights is not None:
                new = weights[0] * flow[c, x + 1] + weights[1] * new
            if ynext is None:
                out[c, x] = new
            else:
                out[c, x + 1] = new
                faces = pack(new, c, x, faces, lane8, ynext)
        return faces

    def body(i, faces):
        for x in (3 * i, 7 - 3 * i, 1 + 4 * i, 2 + 4 * i):
            faces = plane(x, faces)
        if early is not None:
            pl.when(i == 0)(early)
        return faces

    return lax.fori_loop(0, 2, body, jnp.zeros((8, 128), F32))


def pack(new, c, x, faces, lane8, ynext):
    ynext[0, c, pl.ds(x, 1), :] = new[0:1]
    ynext[1, c, pl.ds(x, 1), :] = new[15:16]
    for half in range(2):
        tile = new[8 * half:8 * half + 8]
        spot = 8 * x + 2 * c + half
        faces = jnp.where(lane8 == spot, tile[:, 0:1], faces)
        faces = jnp.where(lane8 == spot + 64, tile[:, 127:128], faces)
    return faces


def comm_kernel(flow, basis, sample_in, result, snaps, upper, inverse, row,
                sample, bt, both, fields, ysend, zsend, ylo, yhi, zlo, zhi,
                scat, r1, piece, r2, mine, full, rowmine, rr1, rowsum, rr2,
                load_sem, ssem, rsem, gsem, know):
    gx, gy, gz = (lax.axis_index(n) for n in ("gx", "gy", "gz"))
    me = gy * GZ + gz

    def plane_id(k):
        other = lax.rem(me + k, PLANE)
        return other, (gx, other // GZ, lax.rem(other, GZ))

    def at(dx=0, dy=0, dz=0):
        return (lax.rem(gx + dx + GX, GX), lax.rem(gy + dy + GY, GY), lax.rem(gz + dz + GZ, GZ))

    def tell(sem, where):
        pl.semaphore_signal(sem, inc=1, device_id=where, device_id_type=MESH)

    barrier = pltpu.get_barrier_semaphore()
    for d in (1, -1):
        tell(barrier, at(dx=d))
    for d in range(1, GY):
        tell(barrier, at(dy=d))
    for d in range(1, GZ):
        tell(barrier, at(dz=d))
    load_bt = pltpu.make_async_copy(basis, bt, load_sem.at[1])
    load_bt.start()
    load = pltpu.make_async_copy(flow, fields.at[0, :, pl.ds(1, 8)], load_sem.at[0])
    load.start()
    load_sample = pltpu.make_async_copy(sample_in, sample, load_sem.at[2])
    load_sample.start()
    load_bt.wait()
    gram = jnp.zeros((128, 128), F32)
    blank = jnp.zeros((1, 256), F32)
    for c in range(3):
        block = jnp.concatenate([bt[c], blank], axis=0)
        gram = gram + times_transposed(block, block)
    for i in range(PLANE):
        scat[i] = gram[4 * i:4 * i + 4]
    load.wait()
    lane8 = iota((8, 128), 1)

    def first(i, faces):
        for d in range(UNROLL):
            x = UNROLL * i + d
            for c in range(4):
                faces = pack(fields[0, c, x + 1], c, x, faces, lane8, ysend.at[0])
        return faces

    zsend[0] = lax.fori_loop(0, 8 // UNROLL, first, jnp.zeros((8, 128), F32))
    pl.semaphore_wait(barrier, 2 + GY - 1 + GZ - 1)
    for d in range(1, GZ):
        tell(know.at[0], at(dz=d))
    for d in (1, -1):
        tell(know.at[1], at(dx=d))

    def moves(s, which=range(6)):
        f = fields.at[s]
        ends = [
            (f.at[:, pl.ds(1, 1)], f.at[:, pl.ds(9, 1)], at(dx=-1)),
            (f.at[:, pl.ds(8, 1)], f.at[:, pl.ds(0, 1)], at(dx=1)),
            (ysend.at[s, 0], yhi.at[s], at(dy=-1)),
            (ysend.at[s, 1], ylo.at[s], at(dy=1)),
            (zsend.at[s], zhi.at[s], at(dz=-1)),
            (zsend.at[s], zlo.at[s], at(dz=1)),
        ]
        return [
            pltpu.make_async_remote_copy(src_ref=ends[i][0], dst_ref=ends[i][1],
                                         send_sem=ssem.at[s, i], recv_sem=rsem.at[s, i],
                                         device_id=ends[i][2], device_id_type=MESH)
            for i in which
        ]

    def exchange(s, which):
        for copy in moves(s, which):
            copy.start()

    def scatter(k, carry):
        other, where = plane_id(k)
        pltpu.make_async_remote_copy(src_ref=scat.at[other], dst_ref=r1.at[me], send_sem=gsem.at[0],
                                     recv_sem=gsem.at[1], device_id=where, device_id_type=MESH).start()
        return carry

    def spread(src, dst, sems, line):
        def go(k, carry):
            where = at(dx=k) if line else plane_id(k)[1]
            pltpu.make_async_remote_copy(src_ref=src, dst_ref=dst.at[gx if line else me],
                                         send_sem=gsem.at[sems], recv_sem=gsem.at[sems + 1],
                                         device_id=where, device_id_type=MESH).start()
            return carry
        lax.fori_loop(1, GX if line else PLANE, go, 0)

    def settle(buf, sem, count):
        part = buf.at[pl.ds(0, count)]
        pltpu.make_async_copy(part, part, gsem.at[sem]).wait()

    def add_up(buf, count):
        parts = [buf[i] for i in range(count)]
        while len(parts) > 1:
            parts = [a + b for a, b in zip(parts[::2], parts[1::2])]
        return parts[0]

    def step(s, dst, weights):
        ynext = ysend.at[s + 1] if s < 2 else None
        early = functools.partial(exchange, s + 1, range(2)) if s < 2 else None
        faces = stencil(fields.at[s], fields.at[0], dst, ylo.at[s], yhi.at[s], zlo.at[s],
                        zhi.at[s], ynext, gy, weights, early)
        if s < 2:
            zsend[s + 1] = faces
            exchange(s + 1, range(2, 6))

    exchange(0, range(6))

    pl.semaphore_wait(know.at[0], GZ - 1)
    lax.fori_loop(1, PLANE, scatter, 0)
    r1[me] = scat[me]
    pl.semaphore_wait(know.at[1], 2)
    for d in (2, -2):
        tell(know.at[2], at(dx=d))

    for c in moves(0):
        c.wait_recv()
    step(0, fields.at[1], None)

    pl.semaphore_wait(know.at[2], 2)
    for d in (4, -4):
        tell(know.at[3], at(dx=d))
    for c in moves(1):
        c.wait_recv()
    settle(r1, 1, PLANE - 1)
    pl.semaphore_wait(know.at[3], 2)
    total = add_up(r1, PLANE)
    piece[...] = total
    spread(piece, r2, 2, True)
    r2[gx] = total

    step(1, fields.at[2], (0.75, 0.25))
    for c in moves(2):
        c.wait_recv()
    step(2, result, (1.0 / 3.0, 2.0 / 3.0))

    load_sample.wait()
    s = sample[...]
    rows = (iota((128, 256), 0) == s // 128).astype(F32)
    cols = iota((128, 256), 0) == lax.rem(s, 128)
    line = jnp.zeros((1, 128), F32)
    for c in range(3):
        velocity = result[c].reshape(128, 128)
        picked = lax.dot_general(velocity, rows, (((0,), (0,)), ((), ())), precision=HIGH,
                                 preferred_element_type=F32)
        snap = jnp.sum(jnp.where(cols, picked, 0.0), axis=0, keepdims=True)
        snaps[c:c + 1] = snap
        block = jnp.concatenate([bt[c], snap], axis=0)
        line = line + times_transposed(jnp.broadcast_to(snap, (8, 256)), block)[0:1]
    rowmine[...] = line
    spread(rowmine, rr1, 6, False)
    rr1[me] = line

    settle(r2, 3, GX - 1)
    total = add_up(r2, GX)
    mine[...] = total
    spread(mine, full, 4, False)
    full[me] = total

    settle(rr1, 7, PLANE - 1)
    total = add_up(rr1, PLANE)
    rowsum[...] = total
    spread(rowsum, rr2, 8, True)
    rr2[gx] = total

    settle(full, 5, PLANE - 1)
    unit = iota((4, 128), 1)
    for i in range(PLANE):
        below = 4 * i + iota((4, 128), 0)
        corner = (below == 127) & (unit == 127)
        both[4 * i:4 * i + 4, :128] = jnp.where(corner, 1.0, full[i] * (1.0 / COUNT))
        both[4 * i:4 * i + 4, 128:] = (unit == below).astype(F32)
    panel = functools.partial(eliminate, both=both, upper=upper, inverse=inverse)
    lax.fori_loop(0, 8, panel, 0)
    settle(rr2, 9, GX - 1)
    row[...] = add_up(rr2, GX)

    for s in range(3):
        for c in moves(s):
            c.wait_send()
    settle(r1, 0, PLANE - 1)
    settle(r2, 2, GX - 1)
    settle(full, 4, PLANE - 1)
    settle(rr1, 6, PLANE - 1)
    settle(rr2, 8, GX - 1)


def pivots(near, start, left, right, later=None):
    full = (8, 128)
    e = [[None] * 8 for _ in range(8)]
    for k in range(8):
        col = jnp.broadcast_to(near[:, start + k:start + k + 1], full)
        for i in range(k, 8):
            e[i][k] = jnp.broadcast_to(col[i:i + 1], full)
    parts = [left, right]
    if later is not None:
        below = [jnp.broadcast_to(later[0][:, start + k:start + k + 1], full) for k in range(8)]
        parts.append(near)
        lows = [later[1], later[2], later[0]]
    rows = [[jnp.broadcast_to(a[i:i + 1], full) for i in range(8)] for a in parts]
    sub = iota(full, 0)
    up, inv = rows[0][0], rows[1][0]
    for k in range(8):
        scale = lax.rsqrt(e[k][k])
        up = jnp.where(sub == k, rows[0][k] * scale, up)
        inv = jnp.where(sub == k, rows[1][k] * scale, inv)
        if k < 7 or later is not None:
            recip = 1.0 / e[k][k]
        for i in range(k + 1, 8):
            part = e[i][k] * recip
            for m in range(k + 1, i + 1):
                e[i][m] = e[i][m] - part * e[m][k]
            for x in rows:
                x[i] = x[i] - part * x[k]
        if later is not None:
            part = below[k] * recip
            for m in range(k + 1, 8):
                below[m] = below[m] - part * e[m][k]
            lows = [low - part * x[k] for low, x in zip(lows, rows)]
    return (up, inv, lows) if later is not None else (up, inv)


def eliminate(b, carry, both, upper, inverse):
    rows = pl.ds(pl.multiple_of(16 * b, 16), 16) if not isinstance(b, int) else pl.ds(16 * b, 16)
    p = both[rows, :]
    left, right = p[:, :128], p[:, 128:]
    near, start = left, 0
    if isinstance(b, int):
        start = 16 * b
    else:
        near = pltpu.roll(left, lax.rem(128 - 16 * b, 128), 1)
    up_a, inv_a, (left_b, right_b, near_b) = pivots(
        near[:8], start, left[:8], right[:8], (near[8:], left[8:], right[8:]))
    up_b, inv_b = pivots(near_b, start + 8, left_b, right_b)
    up = jnp.concatenate([up_a, up_b], axis=0)
    inv = jnp.concatenate([inv_a, inv_b], axis=0)
    up = jnp.where(iota((16, 128), 1) >= 16 * b + iota((16, 128), 0), up, 0.0)
    upper[rows, :] = up
    inverse[rows, :] = inv
    if not isinstance(b, int) or b < 7:
        both[...] = both[...] - lax.dot_general(
            up, jnp.concatenate([up, inv], axis=1), (((0,), (0,)), ((), ())), precision=HIGH,
            preferred_element_type=F32)
    return carry


def times_transposed(a, b):
    return lax.dot_general(a, b, (((1,), (1,)), ((), ())), precision=HIGH,
                           preferred_element_type=F32)


def solve_kernel(bt, snap, upper, inverse, row, flow, out_to, factor_to, flow_to,
                 out, factor, sems):
    stores = []

    def store(a, b):
        stores.append(pltpu.make_async_copy(a, b, sems.at[len(stores)]))
        stores[-1].start()

    store(flow, flow_to)
    lane = iota((8, 128), 1)
    w = inverse[...]
    stacked = [jnp.concatenate([bt[c], snap[c:c + 1]], axis=0) for c in range(3)]
    for c in range(3):
        out[c] = jnp.dot(w, stacked[c], precision=HIGH, preferred_element_type=F32)
    r = jnp.broadcast_to(row[...] * (1.0 / COUNT), (8, 128))
    inner = jnp.where(lane < 127, r, 0.0)
    y = jnp.where(lane < 127, times_transposed(inner, w), 0.0)
    corner = jnp.sum(r - inner, axis=1, keepdims=True) - jnp.sum(y * y, axis=1, keepdims=True)
    scale = lax.rsqrt(corner)
    last = -jnp.dot(y, w, precision=HIGH, preferred_element_type=F32)
    last = jnp.where(lane == 127, 1.0, last) * scale
    edge = jnp.where(lane == 127, corner * scale, y)
    square = jnp.where(iota((128, 128), 1) == 127, jnp.broadcast_to(edge[0:1], (128, 128)).T, upper[...])
    factor[...] = square
    store(factor, factor_to)
    for c in range(3):
        out[c, 127:128] = jnp.dot(last, stacked[c], precision=HIGH,
                                  preferred_element_type=F32)[0:1]
        store(out.at[c], out_to.at[c])
    for copy in stores:
        copy.wait()


def local(flow, basis, sample):
    bt = jnp.transpose(basis, (1, 0, 2))
    vm = pl.BlockSpec(memory_space=pltpu.VMEM)
    hbm = pl.BlockSpec(memory_space=pltpu.HBM)
    square = jax.ShapeDtypeStruct((128, 128), F32)
    whole = jax.ShapeDtypeStruct((4, 8, 16, 128), F32)
    flow_next, snap, upper, inverse, row = pl.pallas_call(
        comm_kernel,
        out_shape=[
            whole,
            jax.ShapeDtypeStruct((3, 256), F32),
            square,
            square,
            jax.ShapeDtypeStruct((1, 128), F32),
        ],
        in_specs=[hbm, hbm, hbm],
        out_specs=[vm] * 5,
        scratch_shapes=[
            pltpu.VMEM((1, 256), jnp.int32),
            pltpu.VMEM((3, 127, 256), F32),
            pltpu.VMEM((128, 256), F32),
            pltpu.VMEM((3, 4, 10, 16, 128), F32),
            pltpu.VMEM((3, 2, 4, 8, 128), F32),
            pltpu.VMEM((3, 8, 128), F32),
            pltpu.VMEM((3, 4, 8, 128), F32),
            pltpu.VMEM((3, 4, 8, 128), F32),
            pltpu.VMEM((3, 8, 128), F32),
            pltpu.VMEM((3, 8, 128), F32),
            pltpu.VMEM((PLANE, 4, 128), F32),
            pltpu.VMEM((PLANE, 4, 128), F32),
            pltpu.VMEM((4, 128), F32),
            pltpu.VMEM((GX, 4, 128), F32),
            pltpu.VMEM((4, 128), F32),
            pltpu.VMEM((PLANE, 4, 128), F32),
            pltpu.VMEM((1, 128), F32),
            pltpu.VMEM((PLANE, 1, 128), F32),
            pltpu.VMEM((1, 128), F32),
            pltpu.VMEM((GX, 1, 128), F32),
            pltpu.SemaphoreType.DMA((3,)),
            pltpu.SemaphoreType.DMA((3, 6)),
            pltpu.SemaphoreType.DMA((3, 6)),
            pltpu.SemaphoreType.DMA((10,)),
            pltpu.SemaphoreType.REGULAR((4,)),
        ],
        compiler_params=pltpu.CompilerParams(collective_id=0, has_side_effects=True,
                                             vmem_limit_bytes=56000000),
    )(flow, bt, sample.reshape(1, 256))
    out, factor, flow_next = pl.pallas_call(
        solve_kernel,
        out_shape=[jax.ShapeDtypeStruct((3, 128, 256), F32), square, whole],
        in_specs=[vm] * 6,
        out_specs=[hbm] * 3,
        scratch_shapes=[
            pltpu.VMEM((3, 128, 256), F32),
            pltpu.VMEM((128, 128), F32),
            pltpu.SemaphoreType.DMA((5,)),
        ],
        compiler_params=pltpu.CompilerParams(vmem_limit_bytes=16 << 20),
    )(bt, snap, upper, inverse, row, flow_next)
    return (flow_next, jnp.transpose(out, (1, 0, 2)), factor)


def solution(mesh):
    return jax.shard_map(
        local,
        mesh=mesh,
        in_specs=(
            P(None, "gx", "gy", "gz"),
            P(None, None, ("gx", "gy", "gz")),
            P(("gx", "gy", "gz")),
        ),
        out_specs=(P(None, "gx", "gy", "gz"), P(None, None, ("gx", "gy", "gz")), P()),
        check_vma=False,
    )
```

```python
import functools

import jax
import jax.numpy as jnp
from jax import lax
from jax.experimental import pallas as pl
from jax.experimental.pallas import tpu as pltpu
from jax.sharding import PartitionSpec as P

DT_STEP = 0.35
VISCOSITY = 0.2
SOUND_SQ = 1.0
DRIVING = 0.5
GX, GY, GZ = 16, 4, 8
PLANE = GY * GZ
UNROLL = 4
COUNT = 3.0 * 256 * GX * GY * GZ
MESH = pl.DeviceIdType.MESH
HIGH = lax.Precision.HIGHEST
F32 = jnp.float32


def iota(shape, dim):
    return lax.broadcasted_iota(jnp.int32, shape, dim)


def stencil(field, flow, out, ylo, yhi, zlo, zhi, ynext, gy, weights, early):
    lane = iota((16, 128), 1)
    lane8 = iota((8, 128), 1)
    row = iota((16, 128), 0)
    low_z, high_z = zlo[...], zhi[...]

    def plane(x, faces):
        zl = pltpu.roll(low_z, 64 - 8 * x, 1)
        zh = pltpu.roll(high_z, (128 - 8 * x) % 128, 1)
        mid = [field[c, x + 1] for c in range(4)]
        sx, sy, sz, lap = [], [], [], []
        for c in range(4):
            a = mid[c]
            xp, xm = field[c, x + 2], field[c, x]
            above = jnp.where(gy < GY - 1, yhi[c, pl.ds(x, 1), :], 0.0)
            below = jnp.where(gy > 0, ylo[c, pl.ds(x, 1), :], 0.0)
            yp = jnp.where(row == 15, above, pltpu.roll(a, 15, 0))
            ym = jnp.where(row == 0, below, pltpu.roll(a, 1, 0))
            m = 2 * c
            left = jnp.concatenate([zl[:, m:m + 1], zl[:, m + 1:m + 2]], axis=0)
            right = jnp.concatenate([zh[:, m:m + 1], zh[:, m + 1:m + 2]], axis=0)
            zp = jnp.where(lane == 127, right, pltpu.roll(a, 127, 1))
            zm = jnp.where(lane == 0, left, pltpu.roll(a, 1, 1))
            sx.append(0.5 * (xp - xm))
            sy.append(0.5 * (yp - ym))
            sz.append(0.5 * (zp - zm))
            if c < 3:
                lap.append(xp + xm + (yp + ym) + (zp + zm) - 6.0 * a)
        press = (sx[3], sy[3], sz[3])
        for c in range(4):
            if c < 3:
                rate = (VISCOSITY * lap[c] - (mid[0] * sx[c] + mid[1] * sy[c] + mid[2] * sz[c])
                        - press[c])
                if c == 0:
                    rate = rate + DRIVING
            else:
                rate = -SOUND_SQ * (sx[0] + sy[1] + sz[2])
            new = mid[c] + DT_STEP * rate
            if weights is not None:
                new = weights[0] * flow[c, x + 1] + weights[1] * new
            if ynext is None:
                out[c, x] = new
            else:
                out[c, x + 1] = new
                faces = pack(new, c, x, faces, lane8, ynext)
        return faces

    def body(i, faces):
        for x in (3 * i, 7 - 3 * i, 1 + 4 * i, 2 + 4 * i):
            faces = plane(x, faces)
        if early is not None:
            pl.when(i == 0)(early)
        return faces

    return lax.fori_loop(0, 2, body, jnp.zeros((8, 128), F32))


def pack(new, c, x, faces, lane8, ynext):
    ynext[0, c, pl.ds(x, 1), :] = new[0:1]
    ynext[1, c, pl.ds(x, 1), :] = new[15:16]
    for half in range(2):
        tile = new[8 * half:8 * half + 8]
        spot = 8 * x + 2 * c + half
        faces = jnp.where(lane8 == spot, tile[:, 0:1], faces)
        faces = jnp.where(lane8 == spot + 64, tile[:, 127:128], faces)
    return faces


def comm_kernel(flow, basis, sample_in, result, snaps, upper, inverse, row,
                sample, bt, both, fields, ysend, zsend, ylo, yhi, zlo, zhi,
                scat, r1, piece, r2, mine, full, rowmine, rr1, rowsum, rr2,
                load_sem, ssem, rsem, gsem, know):
    gx, gy, gz = (lax.axis_index(n) for n in ("gx", "gy", "gz"))
    me = gy * GZ + gz

    def plane_id(k):
        other = lax.rem(me + k, PLANE)
        return other, (gx, other // GZ, lax.rem(other, GZ))

    def at(dx=0, dy=0, dz=0):
        return (lax.rem(gx + dx + GX, GX), lax.rem(gy + dy + GY, GY), lax.rem(gz + dz + GZ, GZ))

    def tell(sem, where):
        pl.semaphore_signal(sem, inc=1, device_id=where, device_id_type=MESH)

    barrier = pltpu.get_barrier_semaphore()
    for d in (1, -1):
        tell(barrier, at(dx=d))
    for d in range(1, GY):
        tell(barrier, at(dy=d))
    for d in range(1, GZ):
        tell(barrier, at(dz=d))
    load_bt = pltpu.make_async_copy(basis, bt, load_sem.at[1])
    load_bt.start()
    load = pltpu.make_async_copy(flow, fields.at[0, :, pl.ds(1, 8)], load_sem.at[0])
    load.start()
    load_sample = pltpu.make_async_copy(sample_in, sample, load_sem.at[2])
    load_sample.start()
    load_bt.wait()
    gram = jnp.zeros((128, 128), F32)
    blank = jnp.zeros((1, 256), F32)
    for c in range(3):
        block = jnp.concatenate([bt[c], blank], axis=0)
        gram = gram + times_transposed(block, block)
    for i in range(PLANE):
        scat[i] = gram[4 * i:4 * i + 4]
    load.wait()
    lane8 = iota((8, 128), 1)

    def first(i, faces):
        for d in range(UNROLL):
            x = UNROLL * i + d
            for c in range(4):
                faces = pack(fields[0, c, x + 1], c, x, faces, lane8, ysend.at[0])
        return faces

    zsend[0] = lax.fori_loop(0, 8 // UNROLL, first, jnp.zeros((8, 128), F32))
    pl.semaphore_wait(barrier, 2 + GY - 1 + GZ - 1)
    for d in range(1, GZ):
        tell(know.at[0], at(dz=d))
    for d in (1, -1):
        tell(know.at[1], at(dx=d))

    def moves(s, which=range(6)):
        f = fields.at[s]
        ends = [
            (f.at[:, pl.ds(1, 1)], f.at[:, pl.ds(9, 1)], at(dx=-1)),
            (f.at[:, pl.ds(8, 1)], f.at[:, pl.ds(0, 1)], at(dx=1)),
            (ysend.at[s, 0], yhi.at[s], at(dy=-1)),
            (ysend.at[s, 1], ylo.at[s], at(dy=1)),
            (zsend.at[s], zhi.at[s], at(dz=-1)),
            (zsend.at[s], zlo.at[s], at(dz=1)),
        ]
        return [
            pltpu.make_async_remote_copy(src_ref=ends[i][0], dst_ref=ends[i][1],
                                         send_sem=ssem.at[s, i], recv_sem=rsem.at[s, i],
                                         device_id=ends[i][2], device_id_type=MESH)
            for i in which
        ]

    def exchange(s, which):
        for copy in moves(s, which):
            copy.start()

    def scatter(k, carry):
        other, where = plane_id(k)
        pltpu.make_async_remote_copy(src_ref=scat.at[other], dst_ref=r1.at[me], send_sem=gsem.at[0],
                                     recv_sem=gsem.at[1], device_id=where, device_id_type=MESH).start()
        return carry

    def spread(src, dst, sems, line):
        def go(k, carry):
            where = at(dx=k) if line else plane_id(k)[1]
            pltpu.make_async_remote_copy(src_ref=src, dst_ref=dst.at[gx if line else me],
                                         send_sem=gsem.at[sems], recv_sem=gsem.at[sems + 1],
                                         device_id=where, device_id_type=MESH).start()
            return carry
        lax.fori_loop(1, GX if line else PLANE, go, 0)

    def settle(buf, sem, count):
        part = buf.at[pl.ds(0, count)]
        pltpu.make_async_copy(part, part, gsem.at[sem]).wait()

    def add_up(buf, count):
        parts = [buf[i] for i in range(count)]
        while len(parts) > 1:
            parts = [a + b for a, b in zip(parts[::2], parts[1::2])]
        return parts[0]

    def step(s, dst, weights):
        ynext = ysend.at[s + 1] if s < 2 else None
        early = functools.partial(exchange, s + 1, range(2)) if s < 2 else None
        faces = stencil(fields.at[s], fields.at[0], dst, ylo.at[s], yhi.at[s], zlo.at[s],
                        zhi.at[s], ynext, gy, weights, early)
        if s < 2:
            zsend[s + 1] = faces
            exchange(s + 1, range(2, 6))

    exchange(0, range(6))

    pl.semaphore_wait(know.at[1], 2)
    for d in (2, -2):
        tell(know.at[2], at(dx=d))
    pl.semaphore_wait(know.at[0], GZ - 1)
    lax.fori_loop(1, PLANE, scatter, 0)
    r1[me] = scat[me]

    for c in moves(0):
        c.wait_recv()
    pl.semaphore_wait(know.at[2], 2)
    for d in (4, -4):
        tell(know.at[3], at(dx=d))
    step(0, fields.at[1], None)

    settle(r1, 1, PLANE - 1)
    pl.semaphore_wait(know.at[3], 2)
    total = add_up(r1, PLANE)
    piece[...] = total
    spread(piece, r2, 2, True)
    r2[gx] = total

    for c in moves(1):
        c.wait_recv()
    step(1, fields.at[2], (0.75, 0.25))
    for c in moves(2):
        c.wait_recv()
    step(2, result, (1.0 / 3.0, 2.0 / 3.0))

    load_sample.wait()
    s = sample[...]
    rows = (iota((128, 256), 0) == s // 128).astype(F32)
    cols = iota((128, 256), 0) == lax.rem(s, 128)
    line = jnp.zeros((1, 128), F32)
    for c in range(3):
        velocity = result[c].reshape(128, 128)
        picked = lax.dot_general(velocity, rows, (((0,), (0,)), ((), ())), precision=HIGH,
                                 preferred_element_type=F32)
        snap = jnp.sum(jnp.where(cols, picked, 0.0), axis=0, keepdims=True)
        snaps[c:c + 1] = snap
        block = jnp.concatenate([bt[c], snap], axis=0)
        line = line + times_transposed(jnp.broadcast_to(snap, (8, 256)), block)[0:1]
    rowmine[...] = line
    spread(rowmine, rr1, 6, False)
    rr1[me] = line

    settle(r2, 3, GX - 1)
    total = add_up(r2, GX)
    mine[...] = total
    spread(mine, full, 4, False)
    full[me] = total

    settle(rr1, 7, PLANE - 1)
    total = add_up(rr1, PLANE)
    rowsum[...] = total
    spread(rowsum, rr2, 8, True)
    rr2[gx] = total

    settle(full, 5, PLANE - 1)
    unit = iota((4, 128), 1)
    for i in range(PLANE):
        below = 4 * i + iota((4, 128), 0)
        corner = (below == 127) & (unit == 127)
        both[4 * i:4 * i + 4, :128] = jnp.where(corner, 1.0, full[i] * (1.0 / COUNT))
        both[4 * i:4 * i + 4, 128:] = (unit == below).astype(F32)
    panel = functools.partial(eliminate, both=both, upper=upper, inverse=inverse)
    lax.fori_loop(0, 8, panel, 0)
    settle(rr2, 9, GX - 1)
    row[...] = add_up(rr2, GX)

    for s in range(3):
        for c in moves(s):
            c.wait_send()
    settle(r1, 0, PLANE - 1)
    settle(r2, 2, GX - 1)
    settle(full, 4, PLANE - 1)
    settle(rr1, 6, PLANE - 1)
    settle(rr2, 8, GX - 1)


def pivots(near, start, left, right, later=None):
    full = (8, 128)
    e = [[None] * 8 for _ in range(8)]
    for k in range(8):
        col = jnp.broadcast_to(near[:, start + k:start + k + 1], full)
        for i in range(k, 8):
            e[i][k] = jnp.broadcast_to(col[i:i + 1], full)
    parts = [left, right]
    if later is not None:
        below = [jnp.broadcast_to(later[0][:, start + k:start + k + 1], full) for k in range(8)]
        parts.append(near)
        lows = [later[1], later[2], later[0]]
    rows = [[jnp.broadcast_to(a[i:i + 1], full) for i in range(8)] for a in parts]
    sub = iota(full, 0)
    up, inv = rows[0][0], rows[1][0]
    for k in range(8):
        scale = lax.rsqrt(e[k][k])
        up = jnp.where(sub == k, rows[0][k] * scale, up)
        inv = jnp.where(sub == k, rows[1][k] * scale, inv)
        if k < 7 or later is not None:
            recip = 1.0 / e[k][k]
        for i in range(k + 1, 8):
            part = e[i][k] * recip
            for m in range(k + 1, i + 1):
                e[i][m] = e[i][m] - part * e[m][k]
            for x in rows:
                x[i] = x[i] - part * x[k]
        if later is not None:
            part = below[k] * recip
            for m in range(k + 1, 8):
                below[m] = below[m] - part * e[m][k]
            lows = [low - part * x[k] for low, x in zip(lows, rows)]
    return (up, inv, lows) if later is not None else (up, inv)


def eliminate(b, carry, both, upper, inverse):
    rows = pl.ds(pl.multiple_of(16 * b, 16), 16) if not isinstance(b, int) else pl.ds(16 * b, 16)
    p = both[rows, :]
    left, right = p[:, :128], p[:, 128:]
    near, start = left, 0
    if isinstance(b, int):
        start = 16 * b
    else:
        near = pltpu.roll(left, lax.rem(128 - 16 * b, 128), 1)
    up_a, inv_a, (left_b, right_b, near_b) = pivots(
        near[:8], start, left[:8], right[:8], (near[8:], left[8:], right[8:]))
    up_b, inv_b = pivots(near_b, start + 8, left_b, right_b)
    up = jnp.concatenate([up_a, up_b], axis=0)
    inv = jnp.concatenate([inv_a, inv_b], axis=0)
    up = jnp.where(iota((16, 128), 1) >= 16 * b + iota((16, 128), 0), up, 0.0)
    upper[rows, :] = up
    inverse[rows, :] = inv
    if not isinstance(b, int) or b < 7:
        both[...] = both[...] - lax.dot_general(
            up, jnp.concatenate([up, inv], axis=1), (((0,), (0,)), ((), ())), precision=HIGH,
            preferred_element_type=F32)
    return carry


def times_transposed(a, b):
    return lax.dot_general(a, b, (((1,), (1,)), ((), ())), precision=HIGH,
                           preferred_element_type=F32)


def solve_kernel(bt, snap, upper, inverse, row, flow, out_to, factor_to, flow_to,
                 out, factor, sems):
    stores = []

    def store(a, b):
        stores.append(pltpu.make_async_copy(a, b, sems.at[len(stores)]))
        stores[-1].start()

    store(flow, flow_to)
    lane = iota((8, 128), 1)
    w = inverse[...]
    stacked = [jnp.concatenate([bt[c], snap[c:c + 1]], axis=0) for c in range(3)]
    for c in range(3):
        out[c] = jnp.dot(w, stacked[c], precision=HIGH, preferred_element_type=F32)
    r = jnp.broadcast_to(row[...] * (1.0 / COUNT), (8, 128))
    inner = jnp.where(lane < 127, r, 0.0)
    y = jnp.where(lane < 127, times_transposed(inner, w), 0.0)
    corner = jnp.sum(r - inner, axis=1, keepdims=True) - jnp.sum(y * y, axis=1, keepdims=True)
    scale = lax.rsqrt(corner)
    last = -jnp.dot(y, w, precision=HIGH, preferred_element_type=F32)
    last = jnp.where(lane == 127, 1.0, last) * scale
    edge = jnp.where(lane == 127, corner * scale, y)
    square = jnp.where(iota((128, 128), 1) == 127, jnp.broadcast_to(edge[0:1], (128, 128)).T, upper[...])
    factor[...] = square
    store(factor, factor_to)
    for c in range(3):
        out[c, 127:128] = jnp.dot(last, stacked[c], precision=HIGH,
                                  preferred_element_type=F32)[0:1]
        store(out.at[c], out_to.at[c])
    for copy in stores:
        copy.wait()


def local(flow, basis, sample):
    bt = jnp.transpose(basis, (1, 0, 2))
    vm = pl.BlockSpec(memory_space=pltpu.VMEM)
    hbm = pl.BlockSpec(memory_space=pltpu.HBM)
    square = jax.ShapeDtypeStruct((128, 128), F32)
    whole = jax.ShapeDtypeStruct((4, 8, 16, 128), F32)
    flow_next, snap, upper, inverse, row = pl.pallas_call(
        comm_kernel,
        out_shape=[
            whole,
            jax.ShapeDtypeStruct((3, 256), F32),
            square,
            square,
            jax.ShapeDtypeStruct((1, 128), F32),
        ],
        in_specs=[hbm, hbm, hbm],
        out_specs=[vm] * 5,
        scratch_shapes=[
            pltpu.VMEM((1, 256), jnp.int32),
            pltpu.VMEM((3, 127, 256), F32),
            pltpu.VMEM((128, 256), F32),
            pltpu.VMEM((3, 4, 10, 16, 128), F32),
            pltpu.VMEM((3, 2, 4, 8, 128), F32),
            pltpu.VMEM((3, 8, 128), F32),
            pltpu.VMEM((3, 4, 8, 128), F32),
            pltpu.VMEM((3, 4, 8, 128), F32),
            pltpu.VMEM((3, 8, 128), F32),
            pltpu.VMEM((3, 8, 128), F32),
            pltpu.VMEM((PLANE, 4, 128), F32),
            pltpu.VMEM((PLANE, 4, 128), F32),
            pltpu.VMEM((4, 128), F32),
            pltpu.VMEM((GX, 4, 128), F32),
            pltpu.VMEM((4, 128), F32),
            pltpu.VMEM((PLANE, 4, 128), F32),
            pltpu.VMEM((1, 128), F32),
            pltpu.VMEM((PLANE, 1, 128), F32),
            pltpu.VMEM((1, 128), F32),
            pltpu.VMEM((GX, 1, 128), F32),
            pltpu.SemaphoreType.DMA((3,)),
            pltpu.SemaphoreType.DMA((3, 6)),
            pltpu.SemaphoreType.DMA((3, 6)),
            pltpu.SemaphoreType.DMA((10,)),
            pltpu.SemaphoreType.REGULAR((4,)),
        ],
        compiler_params=pltpu.CompilerParams(collective_id=0, has_side_effects=True,
                                             vmem_limit_bytes=56000000),
    )(flow, bt, sample.reshape(1, 256))
    out, factor, flow_next = pl.pallas_call(
        solve_kernel,
        out_shape=[jax.ShapeDtypeStruct((3, 128, 256), F32), square, whole],
        in_specs=[vm] * 6,
        out_specs=[hbm] * 3,
        scratch_shapes=[
            pltpu.VMEM((3, 128, 256), F32),
            pltpu.VMEM((128, 128), F32),
            pltpu.SemaphoreType.DMA((5,)),
        ],
        compiler_params=pltpu.CompilerParams(vmem_limit_bytes=16 << 20),
    )(bt, snap, upper, inverse, row, flow_next)
    return (flow_next, jnp.transpose(out, (1, 0, 2)), factor)


def solution(mesh):
    return jax.shard_map(
        local,
        mesh=mesh,
        in_specs=(
            P(None, "gx", "gy", "gz"),
            P(None, None, ("gx", "gy", "gz")),
            P(("gx", "gy", "gz")),
        ),
        out_specs=(P(None, "gx", "gy", "gz"), P(None, None, ("gx", "gy", "gz")), P()),
        check_vma=False,
    )
```

```python
import functools

import jax
import jax.numpy as jnp
from jax import lax
from jax.experimental import pallas as pl
from jax.experimental.pallas import tpu as pltpu
from jax.sharding import PartitionSpec as P

DT_STEP = 0.35
VISCOSITY = 0.2
SOUND_SQ = 1.0
DRIVING = 0.5
GX, GY, GZ = 16, 4, 8
PLANE = GY * GZ
UNROLL = 4
COUNT = 3.0 * 256 * GX * GY * GZ
MESH = pl.DeviceIdType.MESH
HIGH = lax.Precision.HIGHEST
F32 = jnp.float32


def iota(shape, dim):
    return lax.broadcasted_iota(jnp.int32, shape, dim)


def stencil(field, flow, out, ylo, yhi, zlo, zhi, ynext, gy, weights, early):
    lane = iota((16, 128), 1)
    lane8 = iota((8, 128), 1)
    row = iota((16, 128), 0)
    low_z, high_z = zlo[...], zhi[...]

    def plane(x, faces):
        zl = pltpu.roll(low_z, 64 - 8 * x, 1)
        zh = pltpu.roll(high_z, (128 - 8 * x) % 128, 1)
        mid = [field[c, x + 1] for c in range(4)]
        sx, sy, sz, lap = [], [], [], []
        for c in range(4):
            a = mid[c]
            xp, xm = field[c, x + 2], field[c, x]
            above = jnp.where(gy < GY - 1, yhi[c, pl.ds(x, 1), :], 0.0)
            below = jnp.where(gy > 0, ylo[c, pl.ds(x, 1), :], 0.0)
            yp = jnp.where(row == 15, above, pltpu.roll(a, 15, 0))
            ym = jnp.where(row == 0, below, pltpu.roll(a, 1, 0))
            m = 2 * c
            left = jnp.concatenate([zl[:, m:m + 1], zl[:, m + 1:m + 2]], axis=0)
            right = jnp.concatenate([zh[:, m:m + 1], zh[:, m + 1:m + 2]], axis=0)
            zp = jnp.where(lane == 127, right, pltpu.roll(a, 127, 1))
            zm = jnp.where(lane == 0, left, pltpu.roll(a, 1, 1))
            sx.append(0.5 * (xp - xm))
            sy.append(0.5 * (yp - ym))
            sz.append(0.5 * (zp - zm))
            if c < 3:
                lap.append(xp + xm + (yp + ym) + (zp + zm) - 6.0 * a)
        press = (sx[3], sy[3], sz[3])
        for c in range(4):
            if c < 3:
                rate = (VISCOSITY * lap[c] - (mid[0] * sx[c] + mid[1] * sy[c] + mid[2] * sz[c])
                        - press[c])
                if c == 0:
                    rate = rate + DRIVING
            else:
                rate = -SOUND_SQ * (sx[0] + sy[1] + sz[2])
            new = mid[c] + DT_STEP * rate
            if weights is not None:
                new = weights[0] * flow[c, x + 1] + weights[1] * new
            if ynext is None:
                out[c, x] = new
            else:
                out[c, x + 1] = new
                faces = pack(new, c, x, faces, lane8, ynext)
        return faces

    def body(i, faces):
        for x in (3 * i, 7 - 3 * i, 1 + 4 * i, 2 + 4 * i):
            faces = plane(x, faces)
        if early is not None:
            pl.when(i == 0)(early)
        return faces

    return lax.fori_loop(0, 2, body, jnp.zeros((8, 128), F32))


def pack(new, c, x, faces, lane8, ynext):
    ynext[0, c, pl.ds(x, 1), :] = new[0:1]
    ynext[1, c, pl.ds(x, 1), :] = new[15:16]
    for half in range(2):
        tile = new[8 * half:8 * half + 8]
        spot = 8 * x + 2 * c + half
        faces = jnp.where(lane8 == spot, tile[:, 0:1], faces)
        faces = jnp.where(lane8 == spot + 64, tile[:, 127:128], faces)
    return faces


def comm_kernel(flow, basis, sample_in, result, snaps, upper, inverse, row,
                sample, bt, both, fields, ysend, zsend, ylo, yhi, zlo, zhi,
                scat, r1, piece, r2, mine, full, rowmine, rr1, rowsum, rr2,
                load_sem, ssem, rsem, gsem, know):
    gx, gy, gz = (lax.axis_index(n) for n in ("gx", "gy", "gz"))
    me = gy * GZ + gz

    def plane_id(k):
        other = lax.rem(me + k, PLANE)
        return other, (gx, other // GZ, lax.rem(other, GZ))

    def at(dx=0, dy=0, dz=0):
        return (lax.rem(gx + dx + GX, GX), lax.rem(gy + dy + GY, GY), lax.rem(gz + dz + GZ, GZ))

    def tell(sem, where):
        pl.semaphore_signal(sem, inc=1, device_id=where, device_id_type=MESH)

    barrier = pltpu.get_barrier_semaphore()
    for d in (1, -1):
        tell(barrier, at(dx=d))
    for d in range(1, GY):
        tell(barrier, at(dy=d))
    for d in range(1, GZ):
        tell(barrier, at(dz=d))
    load_bt = pltpu.make_async_copy(basis, bt, load_sem.at[1])
    load_bt.start()
    load = pltpu.make_async_copy(flow, fields.at[0, :, pl.ds(1, 8)], load_sem.at[0])
    load.start()
    load_sample = pltpu.make_async_copy(sample_in, sample, load_sem.at[2])
    load_sample.start()
    load_bt.wait()
    gram = jnp.zeros((128, 128), F32)
    blank = jnp.zeros((1, 256), F32)
    for c in range(3):
        block = jnp.concatenate([bt[c], blank], axis=0)
        gram = gram + times_transposed(block, block)
    for i in range(PLANE):
        scat[i] = gram[4 * i:4 * i + 4]
    load.wait()
    lane8 = iota((8, 128), 1)

    def first(i, faces):
        for d in range(UNROLL):
            x = UNROLL * i + d
            for c in range(4):
                faces = pack(fields[0, c, x + 1], c, x, faces, lane8, ysend.at[0])
        return faces

    zsend[0] = lax.fori_loop(0, 8 // UNROLL, first, jnp.zeros((8, 128), F32))
    pl.semaphore_wait(barrier, 2 + GY - 1 + GZ - 1)
    for d in range(1, GZ):
        tell(know.at[0], at(dz=d))
    for d in (1, -1):
        tell(know.at[1], at(dx=d))

    def moves(s, which=range(6)):
        f = fields.at[s]
        ends = [
            (f.at[:, pl.ds(1, 1)], f.at[:, pl.ds(9, 1)], at(dx=-1)),
            (f.at[:, pl.ds(8, 1)], f.at[:, pl.ds(0, 1)], at(dx=1)),
            (ysend.at[s, 0], yhi.at[s], at(dy=-1)),
            (ysend.at[s, 1], ylo.at[s], at(dy=1)),
            (zsend.at[s], zhi.at[s], at(dz=-1)),
            (zsend.at[s], zlo.at[s], at(dz=1)),
        ]
        return [
            pltpu.make_async_remote_copy(src_ref=ends[i][0], dst_ref=ends[i][1],
                                         send_sem=ssem.at[s, i], recv_sem=rsem.at[s, i],
                                         device_id=ends[i][2], device_id_type=MESH)
            for i in which
        ]

    def exchange(s, which):
        for copy in moves(s, which):
            copy.start()

    def far_first(k, count):
        return 1 + lax.rem(k + count // 2 - 4, count - 1)

    def scatter(k, carry):
        other, where = plane_id(far_first(k, PLANE))
        pltpu.make_async_remote_copy(src_ref=scat.at[other], dst_ref=r1.at[me], send_sem=gsem.at[0],
                                     recv_sem=gsem.at[1], device_id=where, device_id_type=MESH).start()
        return carry

    def spread(src, dst, sems, line):
        def go(k, carry):
            k = far_first(k, GX if line else PLANE)
            where = at(dx=k) if line else plane_id(k)[1]
            pltpu.make_async_remote_copy(src_ref=src, dst_ref=dst.at[gx if line else me],
                                         send_sem=gsem.at[sems], recv_sem=gsem.at[sems + 1],
                                         device_id=where, device_id_type=MESH).start()
            return carry
        lax.fori_loop(1, GX if line else PLANE, go, 0)

    def settle(buf, sem, count):
        part = buf.at[pl.ds(0, count)]
        pltpu.make_async_copy(part, part, gsem.at[sem]).wait()

    def add_up(buf, count):
        parts = [buf[i] for i in range(count)]
        while len(parts) > 1:
            parts = [a + b for a, b in zip(parts[::2], parts[1::2])]
        return parts[0]

    def step(s, dst, weights):
        ynext = ysend.at[s + 1] if s < 2 else None
        early = functools.partial(exchange, s + 1, range(2)) if s < 2 else None
        faces = stencil(fields.at[s], fields.at[0], dst, ylo.at[s], yhi.at[s], zlo.at[s],
                        zhi.at[s], ynext, gy, weights, early)
        if s < 2:
            zsend[s + 1] = faces
            exchange(s + 1, range(2, 6))

    exchange(0, range(6))

    pl.semaphore_wait(know.at[1], 2)
    for d in (2, -2):
        tell(know.at[2], at(dx=d))
    pl.semaphore_wait(know.at[0], GZ - 1)
    lax.fori_loop(1, PLANE, scatter, 0)
    r1[me] = scat[me]

    for c in moves(0):
        c.wait_recv()
    pl.semaphore_wait(know.at[2], 2)
    for d in (4, -4):
        tell(know.at[3], at(dx=d))
    step(0, fields.at[1], None)

    settle(r1, 1, PLANE - 1)
    pl.semaphore_wait(know.at[3], 2)
    total = add_up(r1, PLANE)
    piece[...] = total
    spread(piece, r2, 2, True)
    r2[gx] = total

    for c in moves(1):
        c.wait_recv()
    step(1, fields.at[2], (0.75, 0.25))
    for c in moves(2):
        c.wait_recv()
    step(2, result, (1.0 / 3.0, 2.0 / 3.0))

    load_sample.wait()
    s = sample[...]
    rows = (iota((128, 256), 0) == s // 128).astype(F32)
    cols = iota((128, 256), 0) == lax.rem(s, 128)
    line = jnp.zeros((1, 128), F32)
    for c in range(3):
        velocity = result[c].reshape(128, 128)
        picked = lax.dot_general(velocity, rows, (((0,), (0,)), ((), ())), precision=HIGH,
                                 preferred_element_type=F32)
        snap = jnp.sum(jnp.where(cols, picked, 0.0), axis=0, keepdims=True)
        snaps[c:c + 1] = snap
        block = jnp.concatenate([bt[c], snap], axis=0)
        line = line + times_transposed(jnp.broadcast_to(snap, (8, 256)), block)[0:1]
    rowmine[...] = line
    spread(rowmine, rr1, 6, False)
    rr1[me] = line

    settle(r2, 3, GX - 1)
    total = add_up(r2, GX)
    mine[...] = total
    spread(mine, full, 4, False)
    full[me] = total

    settle(rr1, 7, PLANE - 1)
    total = add_up(rr1, PLANE)
    rowsum[...] = total
    spread(rowsum, rr2, 8, True)
    rr2[gx] = total

    settle(full, 5, PLANE - 1)
    unit = iota((4, 128), 1)
    for i in range(PLANE):
        below = 4 * i + iota((4, 128), 0)
        corner = (below == 127) & (unit == 127)
        both[4 * i:4 * i + 4, :128] = jnp.where(corner, 1.0, full[i] * (1.0 / COUNT))
        both[4 * i:4 * i + 4, 128:] = (unit == below).astype(F32)
    panel = functools.partial(eliminate, both=both, upper=upper, inverse=inverse)
    lax.fori_loop(0, 8, panel, 0)
    settle(rr2, 9, GX - 1)
    row[...] = add_up(rr2, GX)

    for s in range(3):
        for c in moves(s):
            c.wait_send()
    settle(r1, 0, PLANE - 1)
    settle(r2, 2, GX - 1)
    settle(full, 4, PLANE - 1)
    settle(rr1, 6, PLANE - 1)
    settle(rr2, 8, GX - 1)


def pivots(near, start, left, right, later=None):
    full = (8, 128)
    e = [[None] * 8 for _ in range(8)]
    for k in range(8):
        col = jnp.broadcast_to(near[:, start + k:start + k + 1], full)
        for i in range(k, 8):
            e[i][k] = jnp.broadcast_to(col[i:i + 1], full)
    parts = [left, right]
    if later is not None:
        below = [jnp.broadcast_to(later[0][:, start + k:start + k + 1], full) for k in range(8)]
        parts.append(near)
        lows = [later[1], later[2], later[0]]
    rows = [[jnp.broadcast_to(a[i:i + 1], full) for i in range(8)] for a in parts]
    sub = iota(full, 0)
    up, inv = rows[0][0], rows[1][0]
    for k in range(8):
        scale = lax.rsqrt(e[k][k])
        up = jnp.where(sub == k, rows[0][k] * scale, up)
        inv = jnp.where(sub == k, rows[1][k] * scale, inv)
        if k < 7 or later is not None:
            recip = 1.0 / e[k][k]
        for i in range(k + 1, 8):
            part = e[i][k] * recip
            for m in range(k + 1, i + 1):
                e[i][m] = e[i][m] - part * e[m][k]
            for x in rows:
                x[i] = x[i] - part * x[k]
        if later is not None:
            part = below[k] * recip
            for m in range(k + 1, 8):
                below[m] = below[m] - part * e[m][k]
            lows = [low - part * x[k] for low, x in zip(lows, rows)]
    return (up, inv, lows) if later is not None else (up, inv)


def eliminate(b, carry, both, upper, inverse):
    rows = pl.ds(pl.multiple_of(16 * b, 16), 16) if not isinstance(b, int) else pl.ds(16 * b, 16)
    p = both[rows, :]
    left, right = p[:, :128], p[:, 128:]
    near, start = left, 0
    if isinstance(b, int):
        start = 16 * b
    else:
        near = pltpu.roll(left, lax.rem(128 - 16 * b, 128), 1)
    up_a, inv_a, (left_b, right_b, near_b) = pivots(
        near[:8], start, left[:8], right[:8], (near[8:], left[8:], right[8:]))
    up_b, inv_b = pivots(near_b, start + 8, left_b, right_b)
    up = jnp.concatenate([up_a, up_b], axis=0)
    inv = jnp.concatenate([inv_a, inv_b], axis=0)
    up = jnp.where(iota((16, 128), 1) >= 16 * b + iota((16, 128), 0), up, 0.0)
    upper[rows, :] = up
    inverse[rows, :] = inv
    if not isinstance(b, int) or b < 7:
        both[...] = both[...] - lax.dot_general(
            up, jnp.concatenate([up, inv], axis=1), (((0,), (0,)), ((), ())), precision=HIGH,
            preferred_element_type=F32)
    return carry


def times_transposed(a, b):
    return lax.dot_general(a, b, (((1,), (1,)), ((), ())), precision=HIGH,
                           preferred_element_type=F32)


def solve_kernel(bt, snap, upper, inverse, row, flow, out_to, factor_to, flow_to,
                 out, factor, sems):
    stores = []

    def store(a, b):
        stores.append(pltpu.make_async_copy(a, b, sems.at[len(stores)]))
        stores[-1].start()

    store(flow, flow_to)
    lane = iota((8, 128), 1)
    w = inverse[...]
    stacked = [jnp.concatenate([bt[c], snap[c:c + 1]], axis=0) for c in range(3)]
    for c in range(3):
        out[c] = jnp.dot(w, stacked[c], precision=HIGH, preferred_element_type=F32)
    r = jnp.broadcast_to(row[...] * (1.0 / COUNT), (8, 128))
    inner = jnp.where(lane < 127, r, 0.0)
    y = jnp.where(lane < 127, times_transposed(inner, w), 0.0)
    corner = jnp.sum(r - inner, axis=1, keepdims=True) - jnp.sum(y * y, axis=1, keepdims=True)
    scale = lax.rsqrt(corner)
    last = -jnp.dot(y, w, precision=HIGH, preferred_element_type=F32)
    last = jnp.where(lane == 127, 1.0, last) * scale
    edge = jnp.where(lane == 127, corner * scale, y)
    square = jnp.where(iota((128, 128), 1) == 127, jnp.broadcast_to(edge[0:1], (128, 128)).T, upper[...])
    factor[...] = square
    store(factor, factor_to)
    for c in range(3):
        out[c, 127:128] = jnp.dot(last, stacked[c], precision=HIGH,
                                  preferred_element_type=F32)[0:1]
        store(out.at[c], out_to.at[c])
    for copy in stores:
        copy.wait()


def local(flow, basis, sample):
    bt = jnp.transpose(basis, (1, 0, 2))
    vm = pl.BlockSpec(memory_space=pltpu.VMEM)
    hbm = pl.BlockSpec(memory_space=pltpu.HBM)
    square = jax.ShapeDtypeStruct((128, 128), F32)
    whole = jax.ShapeDtypeStruct((4, 8, 16, 128), F32)
    flow_next, snap, upper, inverse, row = pl.pallas_call(
        comm_kernel,
        out_shape=[
            whole,
            jax.ShapeDtypeStruct((3, 256), F32),
            square,
            square,
            jax.ShapeDtypeStruct((1, 128), F32),
        ],
        in_specs=[hbm, hbm, hbm],
        out_specs=[vm] * 5,
        scratch_shapes=[
            pltpu.VMEM((1, 256), jnp.int32),
            pltpu.VMEM((3, 127, 256), F32),
            pltpu.VMEM((128, 256), F32),
            pltpu.VMEM((3, 4, 10, 16, 128), F32),
            pltpu.VMEM((3, 2, 4, 8, 128), F32),
            pltpu.VMEM((3, 8, 128), F32),
            pltpu.VMEM((3, 4, 8, 128), F32),
            pltpu.VMEM((3, 4, 8, 128), F32),
            pltpu.VMEM((3, 8, 128), F32),
            pltpu.VMEM((3, 8, 128), F32),
            pltpu.VMEM((PLANE, 4, 128), F32),
            pltpu.VMEM((PLANE, 4, 128), F32),
            pltpu.VMEM((4, 128), F32),
            pltpu.VMEM((GX, 4, 128), F32),
            pltpu.VMEM((4, 128), F32),
            pltpu.VMEM((PLANE, 4, 128), F32),
            pltpu.VMEM((1, 128), F32),
            pltpu.VMEM((PLANE, 1, 128), F32),
            pltpu.VMEM((1, 128), F32),
            pltpu.VMEM((GX, 1, 128), F32),
            pltpu.SemaphoreType.DMA((3,)),
            pltpu.SemaphoreType.DMA((3, 6)),
            pltpu.SemaphoreType.DMA((3, 6)),
            pltpu.SemaphoreType.DMA((10,)),
            pltpu.SemaphoreType.REGULAR((4,)),
        ],
        compiler_params=pltpu.CompilerParams(collective_id=0, has_side_effects=True,
                                             vmem_limit_bytes=56000000),
    )(flow, bt, sample.reshape(1, 256))
    out, factor, flow_next = pl.pallas_call(
        solve_kernel,
        out_shape=[jax.ShapeDtypeStruct((3, 128, 256), F32), square, whole],
        in_specs=[vm] * 6,
        out_specs=[hbm] * 3,
        scratch_shapes=[
            pltpu.VMEM((3, 128, 256), F32),
            pltpu.VMEM((128, 128), F32),
            pltpu.SemaphoreType.DMA((5,)),
        ],
        compiler_params=pltpu.CompilerParams(vmem_limit_bytes=16 << 20),
    )(bt, snap, upper, inverse, row, flow_next)
    return (flow_next, jnp.transpose(out, (1, 0, 2)), factor)


def solution(mesh):
    return jax.shard_map(
        local,
        mesh=mesh,
        in_specs=(
            P(None, "gx", "gy", "gz"),
            P(None, None, ("gx", "gy", "gz")),
            P(("gx", "gy", "gz")),
        ),
        out_specs=(P(None, "gx", "gy", "gz"), P(None, None, ("gx", "gy", "gz")), P()),
        check_vma=False,
    )
```
